32 devices in a mesh: dp: 8 (over z, core), expert: 4 (over y, x).
Axes of the slice: x: 2, y: 2, z: 4, core: 2. Of those that a mesh axis runs over, the one named last changes fastest.
Arguments:
- grads: bfloat16 [4, 16, 1024, 384], P('expert', None, 'dp'), may hold values from -6 to 6
- counts: int32 [4], P('expert'), may hold values from 1 to 15, as said below
Outputs:
- updates: bfloat16 [4, 16, 1024, 384], P('expert', None, 'dp')
The draws below stay inside these ranges and needn't reach their ends.
Inputs may be any that keep to these rules, and one draw needn't show every extreme that they name: Ranks 2k and 2k+1 form pairs: in each pair one rank owns more than 8 matrices, and the pair's two counts sum to at most 16.
All inputs are finite; a program needn't handle non-finite values.
Results may differ from the reference program's by a relative error of at most 0.0058.
Values may be sent and summed in bfloat16 or wider, within the bound.
No kernel may reach another device: no remote copies, remote signals or barrier semaphores. Data moves between devices by JAX's collectives and lax.ppermute only.
A program may use at most 64 MiB of HBM per device.

```python
import math
import jax
import jax.numpy as jnp
from jax import lax

ROWS = 1024
COLS = 384
NS_STEPS = 2
SLOTS = 16
N_EXPERT = 4


def draw_counts(key, part):
    pair_count = N_EXPERT // 2
    key_heavy = jax.random.fold_in(key, 11)
    key_light = jax.random.fold_in(key, 23)
    key_order = jax.random.fold_in(key, 37)
    heavier = jax.random.randint(key_heavy, (pair_count,), SLOTS // 2 + 1, SLOTS)
    pair_ids = jnp.arange(pair_count, dtype=jnp.int32)
    last_pair = pair_ids == pair_count - 1
    heavier = jnp.where(last_pair, SLOTS - 1, heavier)
    spare_room = SLOTS - heavier
    lighter = jax.random.randint(key_light, (pair_count,), 1, spare_room + 1)
    heavy_first = jax.random.randint(key_order, (pair_count,), 0, 2)
    heavy_first = jnp.where(last_pair, 1, heavy_first)
    first_rank = jnp.where(heavy_first == 1, heavier, lighter)
    second_rank = jnp.where(heavy_first == 1, lighter, heavier)
    return jnp.stack([first_rank, second_rank], axis=1).reshape(-1).astype(jnp.int32)


def levels(stream_key, extent, split, low, high):
    gain, own = 1.0, jax.random.fold_in(stream_key, 6)
    for dim, parts in split:
        heights = jnp.exp(jax.random.uniform(jax.random.fold_in(own, dim), (parts,), jnp.float32, low / len(split), high / len(split)))
        gain = gain * jnp.repeat(heights, extent[dim] // parts).reshape([-1 if axis == dim else 1 for axis in range(len(extent))])
    return gain


def scatter_about(stream_key, dims, scale, bound, pieces=(), held_as=jnp.bfloat16):
    values = scale * jax.random.normal(stream_key, dims, jnp.float32)
    if pieces:
        values = values * levels(stream_key, dims, pieces, -0.22, 0.18)
    return jnp.clip(values, -bound, bound).astype(held_as)


def setup_inputs(seed: int = 0) -> dict:
    arg_keys = jax.random.split(jax.random.key(seed), 3)
    grads = scatter_about(arg_keys[0], (N_EXPERT, SLOTS, ROWS, COLS), 1.0, 6.0, ((0, 4), (2, 8)))
    counts = draw_counts(jax.random.fold_in(arg_keys[2], 71), 0)
    return dict(grads=grads, counts=counts)


poly_first = 3.4445
poly_second = -4.775
poly_third = 2.0315

def orthogonalize(matrix):
    values = matrix.astype(jnp.float32)
    frob_norm = jnp.sqrt(jnp.sum(values * values))
    current = (values / (frob_norm + 1e-07)).astype(jnp.bfloat16)
    scale_out = math.sqrt(matrix.shape[0])
    result = jnp.zeros_like(matrix)
    for iteration in range(NS_STEPS):
        gram_matrix = lax.dot_general(current, current, (((0,), (0,)), ((), ())), preferred_element_type=jnp.float32).astype(jnp.bfloat16)
        squared = jnp.dot(gram_matrix, gram_matrix, preferred_element_type=jnp.float32)
        poly_matrix = (poly_second * gram_matrix.astype(jnp.float32) + poly_third * squared).astype(jnp.bfloat16)
        updated = poly_first * current.astype(jnp.float32) + jnp.dot(current, poly_matrix, preferred_element_type=jnp.float32)
        if iteration + 1 < NS_STEPS:
            current = updated.astype(jnp.bfloat16)
        else:
            result = (updated * scale_out).astype(jnp.bfloat16)
    return result

def blank(matrix):
    return jnp.zeros_like(matrix)

def reference(grads, counts):
    flat = grads.reshape(N_EXPERT * SLOTS, ROWS, COLS)
    slot_ids = jnp.arange(SLOTS, dtype=jnp.int32)
    live_flags = (slot_ids[None, :] < counts[:, None]).reshape(-1)

    def handle(item):
        matrix, flag = item
        return lax.cond(flag, orthogonalize, blank, matrix)
    updates = lax.map(handle, (flat, live_flags))
    return updates.reshape(grads.shape)
```

```python
import functools
import math

import jax
import jax.numpy as jnp
from jax import lax
from jax.experimental import pallas as pl
from jax.experimental.pallas import tpu as pltpu
from jax.sharding import PartitionSpec as P

NS_STEPS = 2


poly_first = 3.4445
poly_second = -4.775
poly_third = 2.0315

LANES = 128
CORES = 2
VMEM_LIMIT = 16 << 20

f32 = jnp.float32
bf16 = jnp.bfloat16


def from_partner(block, axis, apart):
    count = lax.axis_size(axis)
    route = []
    for low in range(count):
        high = low | 1 << apart
        if high != low and high < count:
            route += [(low, high), (high, low)]
    return lax.ppermute(block, axis, route)


def orthogonalize(matrix):
    values = matrix.astype(jnp.float32)
    frob_norm = jnp.sqrt(jnp.sum(values * values))
    current = (values / (frob_norm + 1e-07)).astype(jnp.bfloat16)
    scale_out = math.sqrt(matrix.shape[0])
    result = jnp.zeros_like(matrix)
    for iteration in range(NS_STEPS):
        gram_matrix = lax.dot_general(
            current, current, (((0,), (0,)), ((), ())), preferred_element_type=jnp.float32
        ).astype(jnp.bfloat16)
        squared = jnp.dot(gram_matrix, gram_matrix, preferred_element_type=jnp.float32)
        poly_matrix = (poly_second * gram_matrix.astype(jnp.float32) + poly_third * squared).astype(
            jnp.bfloat16
        )
        updated = poly_first * current.astype(jnp.float32) + jnp.dot(
            current, poly_matrix, preferred_element_type=jnp.float32
        )
        if iteration + 1 < NS_STEPS:
            current = updated.astype(jnp.bfloat16)
        else:
            result = (updated * scale_out).astype(jnp.bfloat16)
    return result


def blank(matrix):
    return jnp.zeros_like(matrix)


def strips_to_owners(grads, counts):
    held = grads[0]
    own_count = counts[0]
    total_slots = held.shape[0]
    half_slots = total_slots // 2
    position = lax.axis_index("dp")
    slot_ids = jnp.arange(half_slots, dtype=jnp.int32)
    received, partner_counts = from_partner((held[half_slots:], counts), "expert", 0)
    incoming = jnp.flip(received, 0)
    surplus_in = partner_counts[0] - half_slots
    keep_own = slot_ids < own_count
    balanced = jnp.where(keep_own[:, None, None], held[:half_slots], incoming)
    live_flags = keep_own | (slot_ids >= half_slots - surplus_in)
    gathered = lax.all_to_all(balanced, "dp", split_axis=0, concat_axis=1, tiled=True)
    finished = lax.cond(live_flags[position], orthogonalize, blank, gathered[0])[None]
    restored = lax.all_to_all(finished, "dp", split_axis=1, concat_axis=0, tiled=True)
    returned = from_partner(restored, "expert", 0)
    lower_part = jnp.where(keep_own[:, None, None], restored, jnp.zeros_like(restored))
    upper_keep = slot_ids + half_slots < own_count
    upper_part = jnp.where(
        upper_keep[:, None, None], jnp.flip(returned, 0), jnp.zeros_like(returned)
    )
    result = jnp.concatenate([lower_part, upper_part], axis=0)
    return result[None]


def blocks_of(cols):
    count = cols // LANES
    crossed = [(i, j) for i in range(count) for j in range(i + 1, count)]
    return count, crossed


def packed_rows(cols, chips):
    count, crossed = blocks_of(cols)
    rows = LANES * (len(crossed) + count // 2) + (LANES // 2) * (count % 2)
    spare = -(-(count + 2 * chips) // 16) * 16
    return rows, rows + spare


def grid_of(rows, cols):
    return (
        lax.broadcasted_iota(jnp.int32, (rows, cols), 0),
        lax.broadcasted_iota(jnp.int32, (rows, cols), 1),
    )


def split_kernel(sizes, place_ref, held_ref, *refs):
    n = len(sizes)
    kept, sent, sem = refs[:n], refs[n : 2 * n], refs[2 * n]
    core = place_ref[0]
    copies = []
    start = 0
    for i, size in enumerate(sizes):
        for k, (ref, which) in enumerate(((sent[i], 1 - core), (kept[i], core))):
            copies.append(
                pltpu.make_async_copy(
                    held_ref.at[pl.ds(start + which * size, size)], ref, sem.at[2 * i + k]
                )
            )
        start += CORES * size
    for copy in copies:
        copy.start()
    for copy in copies:
        copy.wait()


def gram_kernel(chips, place_ref, kept_ref, got_ref, out_ref):
    size, _, cols = kept_ref.shape
    count, crossed = blocks_of(cols)
    top, total = packed_rows(cols, chips)
    half = LANES // 2
    row, col = grid_of(LANES, LANES)
    line, _ = grid_of(total - top, LANES)
    chip = place_ref[1]
    for s in range(size):
        x = jnp.concatenate([kept_ref[s], got_ref[s]], axis=0)
        g = lax.dot_general(x, x, (((0,), (0,)), ((), ())), preferred_element_type=f32)

        def block(i, j):
            return g[i * LANES : (i + 1) * LANES, j * LANES : (j + 1) * LANES]

        at = 0
        for i, j in crossed:
            out_ref[s, at : at + LANES, :] = block(i, j).astype(bf16)
            at += LANES
        diagonals = [
            jnp.sum(jnp.where(row == col, block(i, i), 0.0), axis=0, keepdims=True)
            for i in range(count)
        ]
        for i in range(0, count - 1, 2):
            mixed = jnp.where(col >= row, block(i, i), block(i + 1, i + 1))
            out_ref[s, at : at + LANES, :] = mixed.astype(bf16)
            at += LANES
        if count % 2:
            last = block(count - 1, count - 1)
            turned = pltpu.roll(last[half:, :], half, 1)
            mixed = jnp.where(col[:half] >= row[:half], last[:half, :], turned)
            out_ref[s, at : at + half, :] = mixed.astype(bf16)
            at += half
        tail = jnp.zeros((total - top, LANES), f32)
        for i in range(count):
            tail = jnp.where(line == i, diagonals[i], tail)
        trace = sum(diagonals)
        coarse = trace.astype(bf16).astype(f32)
        tail = jnp.where(line == count + 2 * chip, coarse, tail)
        tail = jnp.where(line == count + 2 * chip + 1, trace - coarse, tail)
        out_ref[s, top:, :] = tail.astype(bf16)


def unpack(packed, cols, chips):
    count, crossed = blocks_of(cols)
    top, _ = packed_rows(cols, chips)
    half = LANES // 2
    row, col = grid_of(LANES, LANES)
    tail = packed[top:, :]
    grid = [[None] * count for _ in range(count)]
    at = 0
    for i, j in crossed:
        grid[i][j] = packed[at : at + LANES, :]
        grid[j][i] = grid[i][j].T
        at += LANES
    for i in range(0, count - 1, 2):
        mixed = packed[at : at + LANES, :]
        turned = mixed.T
        grid[i][i] = jnp.where(col >= row, mixed, turned)
        other = jnp.where(col < row, mixed, turned)
        grid[i + 1][i + 1] = jnp.where(col == row, tail[i + 1 : i + 2, :], other)
        at += LANES
    if count % 2:
        i = count - 1
        mixed = packed[at : at + half, :]
        turned = jnp.concatenate([mixed, mixed], axis=0).T
        r, c = row[:half], col[:half]
        upper = jnp.where((c >= r), mixed, turned[:half, :])
        corner = pltpu.roll(jnp.where(c < r, mixed, turned[:half, :]), half, 1)
        corner = jnp.where(c == r + half, tail[i : i + 1, :], corner)
        lower = jnp.where(c < half, turned[half:, :], corner)
        grid[i][i] = jnp.concatenate([upper, lower], axis=0)
    gram = jnp.concatenate([jnp.concatenate(line, axis=1) for line in grid], axis=0)
    trace = jnp.sum(tail[count : count + 2 * chips, :], keepdims=True)
    return gram, trace


def update_kernel(chips, rows, start, place_ref, mine_ref, told_ref, kept_ref, got_ref, out_ref, back_ref):
    size, strip, cols = kept_ref.shape
    core, inner, own_count = place_ref[0], place_ref[2], place_ref[3]
    a, b, c = poly_first, poly_second, poly_third
    dot = functools.partial(jnp.dot, preferred_element_type=f32)
    for s in range(size):
        packed = jnp.where(inner == 1, mine_ref[s].astype(f32), told_ref[s].astype(f32))
        full, trace = unpack(packed, cols, chips)
        gram = full.astype(bf16)
        scale = 1.0 / (jnp.sqrt(trace) + 1e-07)
        square = scale * scale
        poly = ((b * square) * full + (c * square * square) * dot(gram, gram)).astype(bf16)
        once = square * dot(poly, gram)
        second = (a * a * square) * full + (2.0 * a) * once + dot(poly, once.astype(bf16))
        second = second.astype(bf16)
        after = (b * second.astype(f32) + c * dot(second, second)).astype(bf16)
        both = a * (poly.astype(f32) + after.astype(f32)) + dot(poly, after)
        x = jnp.concatenate([kept_ref[s], got_ref[s]], axis=0)
        out = (math.sqrt(rows) * scale) * (a * a * x.astype(f32) + dot(x, both.astype(bf16)))
        live = start + core * size + s < own_count
        out = jnp.where(live, out, 0.0).astype(bf16)
        out_ref[s] = out[:strip]
        back_ref[s] = out[strip:]


def join_kernel(sizes, place_ref, *refs):
    n = len(sizes)
    done, back, out_ref, sem = refs[:n], refs[n : 2 * n], refs[2 * n], refs[2 * n + 1]
    core = place_ref[0]
    copies = []
    start = 0
    for i, size in enumerate(sizes):
        for k, (ref, which) in enumerate(((done[i], core), (back[i], 1 - core))):
            copies.append(
                pltpu.make_async_copy(
                    ref, out_ref.at[0, pl.ds(start + which * size, size)], sem.at[2 * i + k]
                )
            )
        start += CORES * size
    for copy in copies:
        copy.start()
    for copy in copies:
        copy.wait()


SMEM = pl.BlockSpec(memory_space=pltpu.SMEM)
VMEM = pl.BlockSpec(memory_space=pltpu.VMEM)
ANY = pl.BlockSpec(memory_space=pl.ANY)
PARAMS = pltpu.CompilerParams(vmem_limit_bytes=VMEM_LIMIT)


def chunks_of(per_core):
    if per_core < 4:
        return [1] * per_core
    inside = per_core - 2
    return [1] + [2] * (inside // 2) + [1] * (inside % 2) + [1]


def sum_grams(grads, counts):
    held = grads[0]
    slots, strip, cols = held.shape
    devices = lax.axis_size("dp")
    chips = devices // CORES
    position = lax.axis_index("dp")
    core, chip = position % CORES, position // CORES
    middle = chips // 2
    inner = (chip == middle - 1) | (chip == middle)
    place = jnp.stack([core, chip, inner.astype(jnp.int32), counts[0]]).astype(jnp.int32)
    _, total = packed_rows(cols, chips)
    sizes = chunks_of(slots // CORES)

    def along(pairs):
        return [(CORES * i + k, CORES * j + k) for i, j in pairs for k in range(CORES)]

    swap = [(i, i ^ 1) for i in range(devices)]
    inward = [along([(d, d + 1), (chips - 1 - d, chips - 2 - d)]) for d in range(middle - 1)]
    across = along([(middle - 1, middle), (middle, middle - 1)])
    outward = [[(j, i) for i, j in hop] for hop in reversed(inward)]

    piece = [jax.ShapeDtypeStruct((size, strip, cols), bf16) for size in sizes]
    parts = pl.pallas_call(
        functools.partial(split_kernel, sizes),
        out_shape=piece + piece,
        in_specs=[SMEM, ANY],
        out_specs=[VMEM] * (2 * len(sizes)),
        scratch_shapes=[pltpu.SemaphoreType.DMA((2 * len(sizes),))],
        compiler_params=PARAMS,
        name="split",
    )(place, held)
    kept, sent = parts[: len(sizes)], parts[len(sizes) :]
    got = [lax.ppermute(block, "dp", swap) for block in sent]

    def cost(flops, moved):
        return pl.CostEstimate(flops=int(flops), bytes_accessed=int(moved), transcendentals=0)

    done, back = [], []
    start = 0
    for i, size in enumerate(sizes):
        packed = jax.ShapeDtypeStruct((size, total, LANES), bf16)
        gram = pl.pallas_call(
            functools.partial(gram_kernel, chips),
            out_shape=packed,
            in_specs=[SMEM, VMEM, VMEM],
            out_specs=VMEM,
            compiler_params=PARAMS,
            cost_estimate=cost(4 * size * strip * cols * cols, 4 * size * strip * cols),
            name=f"gram{i}",
        )(place, kept[i], got[i])
        for hop in inward:
            gram = gram + lax.ppermute(gram, "dp", hop)
        gram = gram + lax.ppermute(gram, "dp", across)
        told = gram
        for hop in outward:
            came = lax.ppermute(told, "dp", hop)
            if len(outward) > 1:
                reached = functools.reduce(
                    jnp.logical_or, [position == j for _, j in hop], jnp.zeros((), bool)
                )
                told = jnp.where(reached, came, told)
            else:
                told = came
        out, give = pl.pallas_call(
            functools.partial(update_kernel, chips, strip * devices, start),
            out_shape=[piece[i], piece[i]],
            in_specs=[SMEM, VMEM, VMEM, VMEM, VMEM],
            out_specs=[VMEM, VMEM],
            compiler_params=PARAMS,
            cost_estimate=cost(10 * size * cols**3 + 4 * size * strip * cols * cols, 8 * size * strip * cols),
            name=f"update{i}",
        )(place, gram, told, kept[i], got[i])
        done.append(out)
        back.append(lax.ppermute(give, "dp", swap))
        start += CORES * size
    return pl.pallas_call(
        functools.partial(join_kernel, sizes),
        out_shape=jax.ShapeDtypeStruct((1,) + held.shape, bf16),
        in_specs=[SMEM] + [VMEM] * (2 * len(sizes)),
        out_specs=ANY,
        scratch_shapes=[pltpu.SemaphoreType.DMA((2 * len(sizes),))],
        compiler_params=PARAMS,
        name="join",
    )(place, *done, *back)


def per_device(grads, counts):
    _, slots, strip, cols = grads.shape
    devices = lax.axis_size("dp")
    fits = cols % LANES == 0 and slots % CORES == 0 and devices % (2 * CORES) == 0
    if fits and CORES * strip * cols >= packed_rows(cols, devices // CORES)[1] * LANES:
        return sum_grams(grads, counts)
    return strips_to_owners(grads, counts)


def solution(mesh):
    placed = (P("expert", None, "dp", None), P("expert"))
    return jax.shard_map(
        per_device,
        mesh=mesh,
        in_specs=placed,
        out_specs=P("expert", None, "dp", None),
        check_vma=False,
    )
```

```python
import functools
import math

import jax
import jax.numpy as jnp
from jax import lax
from jax.experimental import pallas as pl
from jax.experimental.pallas import tpu as pltpu
from jax.sharding import PartitionSpec as P


NS_STEPS = 2


poly_first = 3.4445
poly_second = -4.775
poly_third = 2.0315

LANES = 128
CORES = 2
VMEM_LIMIT = 16 << 20

f32 = jnp.float32
bf16 = jnp.bfloat16


def from_partner(block, axis, apart):
    count = lax.axis_size(axis)
    route = []
    for low in range(count):
        high = low | 1 << apart
        if high != low and high < count:
            route += [(low, high), (high, low)]
    return lax.ppermute(block, axis, route)


def orthogonalize(matrix):
    values = matrix.astype(jnp.float32)
    frob_norm = jnp.sqrt(jnp.sum(values * values))
    current = (values / (frob_norm + 1e-07)).astype(jnp.bfloat16)
    scale_out = math.sqrt(matrix.shape[0])
    result = jnp.zeros_like(matrix)
    for iteration in range(NS_STEPS):
        gram_matrix = lax.dot_general(
            current, current, (((0,), (0,)), ((), ())), preferred_element_type=jnp.float32
        ).astype(jnp.bfloat16)
        squared = jnp.dot(gram_matrix, gram_matrix, preferred_element_type=jnp.float32)
        poly_matrix = (poly_second * gram_matrix.astype(jnp.float32) + poly_third * squared).astype(
            jnp.bfloat16
        )
        updated = poly_first * current.astype(jnp.float32) + jnp.dot(
            current, poly_matrix, preferred_element_type=jnp.float32
        )
        if iteration + 1 < NS_STEPS:
            current = updated.astype(jnp.bfloat16)
        else:
            result = (updated * scale_out).astype(jnp.bfloat16)
    return result


def blank(matrix):
    return jnp.zeros_like(matrix)


def strips_to_owners(grads, counts):
    held = grads[0]
    own_count = counts[0]
    total_slots = held.shape[0]
    half_slots = total_slots // 2
    position = lax.axis_index("dp")
    slot_ids = jnp.arange(half_slots, dtype=jnp.int32)
    received, partner_counts = from_partner((held[half_slots:], counts), "expert", 0)
    incoming = jnp.flip(received, 0)
    surplus_in = partner_counts[0] - half_slots
    keep_own = slot_ids < own_count
    balanced = jnp.where(keep_own[:, None, None], held[:half_slots], incoming)
    live_flags = keep_own | (slot_ids >= half_slots - surplus_in)
    gathered = lax.all_to_all(balanced, "dp", split_axis=0, concat_axis=1, tiled=True)
    finished = lax.cond(live_flags[position], orthogonalize, blank, gathered[0])[None]
    restored = lax.all_to_all(finished, "dp", split_axis=1, concat_axis=0, tiled=True)
    returned = from_partner(restored, "expert", 0)
    lower_part = jnp.where(keep_own[:, None, None], restored, jnp.zeros_like(restored))
    upper_keep = slot_ids + half_slots < own_count
    upper_part = jnp.where(
        upper_keep[:, None, None], jnp.flip(returned, 0), jnp.zeros_like(returned)
    )
    result = jnp.concatenate([lower_part, upper_part], axis=0)
    return result[None]


def blocks_of(cols):
    count = cols // LANES
    crossed = [(i, j) for i in range(count) for j in range(i + 1, count)]
    return count, crossed


def packed_rows(cols, chips):
    count, crossed = blocks_of(cols)
    rows = LANES * (len(crossed) + count // 2) + (LANES // 2) * (count % 2)
    spare = -(-(count + 2 * chips) // 16) * 16
    return rows, rows + spare


def grid_of(rows, cols):
    return (
        lax.broadcasted_iota(jnp.int32, (rows, cols), 0),
        lax.broadcasted_iota(jnp.int32, (rows, cols), 1),
    )


def split_kernel(groups, place_ref, held_ref, *refs):
    n = len(groups)
    kept, sent, sem = refs[:n], refs[n : 2 * n], refs[2 * n]
    core = place_ref[0]
    copies = []
    for i, group in enumerate(groups):
        for ref, which in ((sent[i], 1 - core), (kept[i], core)):
            for k, (base, step) in enumerate(group):
                copies.append(
                    pltpu.make_async_copy(held_ref.at[base + step * which], ref.at[k], sem.at[len(copies)])
                )
    for copy in copies:
        copy.start()
    for copy in copies:
        copy.wait()


def gram_kernel(chips, group, place_ref, kept_ref, got_ref, *out_refs):
    size, _, cols = kept_ref.shape
    count, crossed = blocks_of(cols)
    top, total = packed_rows(cols, chips)
    half = LANES // 2
    row, col = grid_of(LANES, LANES)
    line, _ = grid_of(total - top, LANES)
    chip = place_ref[1]
    for s in range(size):
        x = jnp.concatenate([kept_ref[s], got_ref[s]], axis=0)
        base, step = group[s]
        live = base + step * place_ref[0] < place_ref[3]
        x = jnp.where(live, x, jnp.zeros_like(x))
        g = lax.dot_general(x, x, (((0,), (0,)), ((), ())), preferred_element_type=f32)

        def block(i, j):
            return g[i * LANES : (i + 1) * LANES, j * LANES : (j + 1) * LANES]

        at = 0
        for i, j in crossed:
            out_refs[s][at : at + LANES, :] = block(i, j).astype(bf16)
            at += LANES
        diagonals = [
            jnp.sum(jnp.where(row == col, block(i, i), 0.0), axis=0, keepdims=True)
            for i in range(count)
        ]
        for i in range(0, count - 1, 2):
            mixed = jnp.where(col >= row, block(i, i), block(i + 1, i + 1))
            out_refs[s][at : at + LANES, :] = mixed.astype(bf16)
            at += LANES
        if count % 2:
            last = block(count - 1, count - 1)
            turned = pltpu.roll(last[half:, :], half, 1)
            mixed = jnp.where(col[:half] >= row[:half], last[:half, :], turned)
            out_refs[s][at : at + half, :] = mixed.astype(bf16)
            at += half
        tail = jnp.zeros((total - top, LANES), f32)
        for i in range(count):
            tail = jnp.where(line == i, diagonals[i], tail)
        trace = sum(diagonals)
        coarse = trace.astype(bf16).astype(f32)
        tail = jnp.where(line == count + 2 * chip, coarse, tail)
        tail = jnp.where(line == count + 2 * chip + 1, trace - coarse, tail)
        out_refs[s][top:, :] = tail.astype(bf16)


def unpack(packed, cols, chips):
    count, crossed = blocks_of(cols)
    top, _ = packed_rows(cols, chips)
    half = LANES // 2
    row, col = grid_of(LANES, LANES)
    tail = packed[top:, :]
    grid = [[None] * count for _ in range(count)]
    at = 0
    for i, j in crossed:
        grid[i][j] = packed[at : at + LANES, :]
        grid[j][i] = grid[i][j].T
        at += LANES
    for i in range(0, count - 1, 2):
        mixed = packed[at : at + LANES, :]
        turned = mixed.T
        grid[i][i] = jnp.where(col >= row, mixed, turned)
        other = jnp.where(col < row, mixed, turned)
        grid[i + 1][i + 1] = jnp.where(col == row, tail[i + 1 : i + 2, :], other)
        at += LANES
    if count % 2:
        i = count - 1
        mixed = packed[at : at + half, :].astype(f32)
        turned = jnp.concatenate([mixed, mixed], axis=0).T
        r, c = row[:half], col[:half]
        upper = jnp.where(c >= r, mixed, turned[:half, :])
        corner = pltpu.roll(jnp.where(c < r, mixed, turned[:half, :]), half, 1)
        corner = jnp.where(c == r + half, tail[i : i + 1, :].astype(f32), corner)
        lower = jnp.where(c < half, turned[half:, :], corner)
        grid[i][i] = jnp.concatenate([upper, lower], axis=0).astype(bf16)
    gram = jnp.concatenate([jnp.concatenate(line, axis=1) for line in grid], axis=0)
    trace = jnp.sum(tail[count : count + 2 * chips, :].astype(f32), keepdims=True)
    return gram, trace


def update_kernel(chips, rows, slots, places, place_ref, *refs):
    n = len(slots)
    mine, told, kept, got = (refs[i * n : (i + 1) * n] for i in range(4))
    out_ref, back_ref = refs[4 * n :]
    _, strip, cols = kept[0].shape
    core, inner, own_count = place_ref[0], place_ref[2], place_ref[3]
    a, b, c = poly_first, poly_second, poly_third
    dot = functools.partial(jnp.dot, preferred_element_type=f32)
    span = range(n)
    gram, scale = [], []
    for k in span:
        full, trace = unpack(jnp.where(inner == 1, mine[k][...], told[k][...]), cols, chips)
        gram.append(full)
        scale.append(1.0 / (jnp.sqrt(trace) + 1e-07))
    square = [v * v for v in scale]
    product = [dot(g, g) for g in gram]
    poly = [
        ((b * square[k]) * gram[k].astype(f32) + (c * square[k] * square[k]) * product[k]).astype(bf16)
        for k in span
    ]
    x = [jnp.concatenate([kept[k][places[k]], got[k][places[k]]], axis=0) for k in span]
    once = [square[k] * dot(poly[k], gram[k]) for k in span]
    current = [(a * x[k].astype(f32) + dot(x[k], poly[k])).astype(bf16) for k in span]
    twice = [dot(poly[k], once[k].astype(bf16)) for k in span]
    second = [
        ((a * a * square[k]) * gram[k].astype(f32) + (2.0 * a) * once[k] + twice[k]).astype(bf16)
        for k in span
    ]
    product = [dot(g, g) for g in second]
    poly = [(b * second[k].astype(f32) + c * product[k]).astype(bf16) for k in span]
    for k in span:
        out = a * current[k].astype(f32) + dot(current[k], poly[k])
        live = slots[k][0] + core * slots[k][1] < own_count
        out = jnp.where(live, (math.sqrt(rows) * scale[k]) * out, 0.0).astype(bf16)
        out_ref[k] = out[:strip]
        back_ref[k] = out[strip:]


def join_kernel(calls, place_ref, *refs):
    n = len(calls)
    done, back, out_ref, sem = refs[:n], refs[n : 2 * n], refs[2 * n], refs[2 * n + 1]
    core = place_ref[0]
    copies = []
    for i, call in enumerate(calls):
        for ref, which in ((done[i], core), (back[i], 1 - core)):
            for k, (base, step) in enumerate(call):
                copies.append(
                    pltpu.make_async_copy(ref.at[k], out_ref.at[0, base + step * which], sem.at[len(copies)])
                )
    for copy in copies:
        copy.start()
    for copy in copies:
        copy.wait()


SMEM = pl.BlockSpec(memory_space=pltpu.SMEM)
VMEM = pl.BlockSpec(memory_space=pltpu.VMEM)
ANY = pl.BlockSpec(memory_space=pl.ANY)
HBM = pl.BlockSpec(memory_space=pltpu.HBM)
PARAMS = pltpu.CompilerParams(vmem_limit_bytes=VMEM_LIMIT)


SLOTS = 16
CHUNKS = ((4, 1), (6, 1), (2, 1), (0, 1), (8, 1), (10, 1))
PASSED = {2: (13, -1), 3: (15, -1)}
GROUPS = ((0, -2), (1, 2, -3, 3), (4, 5))
CALLS = ((0, 1), (2, 3), (-2, 4), (-3, 5))
LAG = 4


def slot_of(k):
    return CHUNKS[k] if k >= 0 else PASSED[-k]


def sum_grams(grads, counts):
    held = grads[0]
    slots, strip, cols = held.shape
    devices = lax.axis_size("dp")
    chips = devices // CORES
    position = lax.axis_index("dp")
    core, chip = position % CORES, position // CORES
    inner = (chip == 1) | (chip == 2)
    place = jnp.stack([core, chip, inner.astype(jnp.int32), counts[0]]).astype(jnp.int32)
    _, total = packed_rows(cols, chips)
    chunks = len(CHUNKS)

    def along(pairs):
        return [(CORES * i + k, CORES * j + k) for i, j in pairs for k in range(CORES)]

    swap = [(i, i ^ 1) for i in range(devices)]
    beside = along([(0, 1), (1, 0), (2, 3), (3, 2)])
    across = along([(1, 2), (2, 1)]) + [(i, i ^ 1) for i in (0, 1, devices - 2, devices - 1)]
    partner = [(i, i ^ 1) for i in range(lax.axis_size("expert"))]

    def cost(flops, moved):
        return pl.CostEstimate(flops=int(flops), bytes_accessed=int(moved), transcendentals=0)

    groups = [[slot_of(k) for k in group] for group in GROUPS]
    piece = [jax.ShapeDtypeStruct((len(group), strip, cols), bf16) for group in groups]
    parts = pl.pallas_call(
        functools.partial(split_kernel, groups),
        out_shape=piece + piece,
        in_specs=[SMEM, HBM],
        out_specs=[VMEM] * (2 * len(groups)),
        scratch_shapes=[pltpu.SemaphoreType.DMA((slots,))],
        compiler_params=PARAMS,
        name="split",
    )(place, pltpu.with_memory_space_constraint(held, pltpu.HBM))
    kept, sent = parts[: len(groups)], parts[len(groups) :]
    got, gram, where = [], {}, {}
    for i, group in enumerate(groups):
        size = len(group)
        got.append(lax.ppermute(sent[i], "dp", swap))
        outs = pl.pallas_call(
            functools.partial(gram_kernel, chips, group),
            out_shape=[jax.ShapeDtypeStruct((total, LANES), bf16)] * size,
            in_specs=[SMEM, VMEM, VMEM],
            out_specs=[VMEM] * size,
            compiler_params=PARAMS,
            cost_estimate=cost(4 * size * strip * cols * cols, 4 * size * strip * cols),
            name="gram",
        )(place, kept[i], got[i])
        for k, name in enumerate(GROUPS[i]):
            gram[name], where[name] = outs[k], (i, k)
    for k in PASSED:
        came = lax.ppermute(gram[-k], "expert", partner)
        gram[k] = gram[k] + came

    def chosen(one, other):
        return lax.select(jnp.broadcast_to(inner, one.shape), one, other)

    full, told, half = {}, {}, {}
    for t in range(chunks + LAG):
        k = t - LAG
        if k >= 0:
            came = lax.ppermute(half[k], "dp", across)
            full[k] = half[k] + came
        if k < 0:
            load = gram[t]
        elif t < chunks:
            load = chosen(full[k], gram[t])
        else:
            load = full[k]
        came = lax.ppermute(load, "dp", beside)
        if t < chunks:
            half[t] = gram[t] + came
        if k >= 0:
            told[k] = came
    for k in PASSED:
        load = chosen(full[k], told[k])
        full[-k] = told[-k] = lax.ppermute(load, "expert", partner)

    done, back = [], []
    for call in CALLS:
        n = len(call)
        out = jax.ShapeDtypeStruct((n, strip, cols), bf16)
        out, give = pl.pallas_call(
            functools.partial(
                update_kernel,
                chips,
                strip * devices,
                [slot_of(k) for k in call],
                [where[k][1] for k in call],
            ),
            out_shape=[out, out],
            in_specs=[SMEM] + [VMEM] * (4 * n),
            out_specs=[VMEM, VMEM],
            compiler_params=PARAMS,
            cost_estimate=cost(8 * n * cols**3 + 8 * n * strip * cols * cols, 8 * n * strip * cols),
            name="update",
        )(
            place,
            *[full[k] for k in call],
            *[told[k] for k in call],
            *[kept[where[k][0]] for k in call],
            *[got[where[k][0]] for k in call],
        )
        done.append(out)
        back.append(lax.ppermute(give, "dp", swap))
    calls = [[slot_of(k) for k in call] for call in CALLS]
    return pl.pallas_call(
        functools.partial(join_kernel, calls),
        out_shape=jax.ShapeDtypeStruct((1,) + held.shape, bf16),
        in_specs=[SMEM] + [VMEM] * (2 * len(calls)),
        out_specs=ANY,
        scratch_shapes=[pltpu.SemaphoreType.DMA((slots,))],
        compiler_params=PARAMS,
        name="join",
    )(place, *done, *back)


def solution(mesh):
    placed = (P("expert", None, "dp", None), P("expert"))
    devices = mesh.shape["dp"]

    def step(grads, counts):
        _, slots, rows, cols = grads.shape
        strip = rows // devices
        summed = devices == 4 * CORES and cols % LANES == 0 and slots == SLOTS and mesh.shape["expert"] % 2 == 0
        summed = summed and CORES * strip * cols >= packed_rows(cols, devices // CORES)[1] * LANES

        def per_device(grads, counts):
            return (sum_grams if summed else strips_to_owners)(grads, counts)

        mapped = jax.shard_map(
            per_device,
            mesh=mesh,
            in_specs=placed,
            out_specs=P("expert", None, "dp", None),
            check_vma=False,
        )
        return mapped(grads, counts)

    return step
```

```python
import functools
import math

import jax
import jax.numpy as jnp
from jax import lax
from jax.experimental import pallas as pl
from jax.experimental.pallas import tpu as pltpu
from jax.sharding import PartitionSpec as P


NS_STEPS = 2


poly_first = 3.4445
poly_second = -4.775
poly_third = 2.0315

LANES = 128
CORES = 2
VMEM_LIMIT = 16 << 20

f32 = jnp.float32
bf16 = jnp.bfloat16


def from_partner(block, axis, apart):
    count = lax.axis_size(axis)
    route = []
    for low in range(count):
        high = low | 1 << apart
        if high != low and high < count:
            route += [(low, high), (high, low)]
    return lax.ppermute(block, axis, route)


def orthogonalize(matrix):
    values = matrix.astype(jnp.float32)
    frob_norm = jnp.sqrt(jnp.sum(values * values))
    current = (values / (frob_norm + 1e-07)).astype(jnp.bfloat16)
    scale_out = math.sqrt(matrix.shape[0])
    result = jnp.zeros_like(matrix)
    for iteration in range(NS_STEPS):
        gram_matrix = lax.dot_general(
            current, current, (((0,), (0,)), ((), ())), preferred_element_type=jnp.float32
        ).astype(jnp.bfloat16)
        squared = jnp.dot(gram_matrix, gram_matrix, preferred_element_type=jnp.float32)
        poly_matrix = (poly_second * gram_matrix.astype(jnp.float32) + poly_third * squared).astype(
            jnp.bfloat16
        )
        updated = poly_first * current.astype(jnp.float32) + jnp.dot(
            current, poly_matrix, preferred_element_type=jnp.float32
        )
        if iteration + 1 < NS_STEPS:
            current = updated.astype(jnp.bfloat16)
        else:
            result = (updated * scale_out).astype(jnp.bfloat16)
    return result


def blank(matrix):
    return jnp.zeros_like(matrix)


def strips_to_owners(grads, counts):
    held = grads[0]
    own_count = counts[0]
    total_slots = held.shape[0]
    half_slots = total_slots // 2
    position = lax.axis_index("dp")
    slot_ids = jnp.arange(half_slots, dtype=jnp.int32)
    received, partner_counts = from_partner((held[half_slots:], counts), "expert", 0)
    incoming = jnp.flip(received, 0)
    surplus_in = partner_counts[0] - half_slots
    keep_own = slot_ids < own_count
    balanced = jnp.where(keep_own[:, None, None], held[:half_slots], incoming)
    live_flags = keep_own | (slot_ids >= half_slots - surplus_in)
    gathered = lax.all_to_all(balanced, "dp", split_axis=0, concat_axis=1, tiled=True)
    finished = lax.cond(live_flags[position], orthogonalize, blank, gathered[0])[None]
    restored = lax.all_to_all(finished, "dp", split_axis=1, concat_axis=0, tiled=True)
    returned = from_partner(restored, "expert", 0)
    lower_part = jnp.where(keep_own[:, None, None], restored, jnp.zeros_like(restored))
    upper_keep = slot_ids + half_slots < own_count
    upper_part = jnp.where(
        upper_keep[:, None, None], jnp.flip(returned, 0), jnp.zeros_like(returned)
    )
    result = jnp.concatenate([lower_part, upper_part], axis=0)
    return result[None]


def blocks_of(cols):
    count = cols // LANES
    crossed = [(i, j) for i in range(count) for j in range(i + 1, count)]
    return count, crossed


def packed_rows(cols, chips):
    count, crossed = blocks_of(cols)
    rows = LANES * (len(crossed) + count // 2) + (LANES // 2) * (count % 2)
    spare = -(-(count + 2 * chips) // 16) * 16
    return rows, rows + spare


def grid_of(rows, cols):
    return (
        lax.broadcasted_iota(jnp.int32, (rows, cols), 0),
        lax.broadcasted_iota(jnp.int32, (rows, cols), 1),
    )


def split_kernel(groups, place_ref, held_ref, *refs):
    n = len(groups)
    kept, sent, sem = refs[:n], refs[n : 2 * n], refs[2 * n]
    core = place_ref[0]
    copies = []
    for i, group in enumerate(groups):
        for ref, which in ((sent[i], 1 - core), (kept[i], core)):
            for k, (base, step) in enumerate(group):
                copies.append(
                    pltpu.make_async_copy(held_ref.at[base + step * which], ref.at[k], sem.at[len(copies)])
                )
    for copy in copies:
        copy.start()
    for copy in copies:
        copy.wait()


def gram_kernel(chips, group, place_ref, counts_ref, kept_ref, got_ref, *out_refs):
    size, _, cols = kept_ref.shape
    count, crossed = blocks_of(cols)
    top, total = packed_rows(cols, chips)
    half = LANES // 2
    row, col = grid_of(LANES, LANES)
    line, _ = grid_of(total - top, LANES)
    chip = place_ref[1]
    for s in range(size):
        x = jnp.concatenate([kept_ref[s], got_ref[s]], axis=0)
        base, step = group[s]
        live = base + step * place_ref[0] < counts_ref[0]
        x = jnp.where(live, x, jnp.zeros_like(x))
        g = lax.dot_general(x, x, (((0,), (0,)), ((), ())), preferred_element_type=f32)

        def block(i, j):
            return g[i * LANES : (i + 1) * LANES, j * LANES : (j + 1) * LANES]

        at = 0
        for i, j in crossed:
            out_refs[s][at : at + LANES, :] = block(i, j).astype(bf16)
            at += LANES
        diagonals = [
            jnp.sum(jnp.where(row == col, block(i, i), 0.0), axis=0, keepdims=True)
            for i in range(count)
        ]
        for i in range(0, count - 1, 2):
            mixed = jnp.where(col >= row, block(i, i), block(i + 1, i + 1))
            out_refs[s][at : at + LANES, :] = mixed.astype(bf16)
            at += LANES
        if count % 2:
            last = block(count - 1, count - 1)
            turned = pltpu.roll(last[half:, :], half, 1)
            mixed = jnp.where(col[:half] >= row[:half], last[:half, :], turned)
            out_refs[s][at : at + half, :] = mixed.astype(bf16)
            at += half
        tail = jnp.zeros((total - top, LANES), f32)
        for i in range(count):
            tail = jnp.where(line == i, diagonals[i], tail)
        trace = sum(diagonals)
        coarse = trace.astype(bf16).astype(f32)
        tail = jnp.where(line == count + 2 * chip, coarse, tail)
        tail = jnp.where(line == count + 2 * chip + 1, trace - coarse, tail)
        out_refs[s][top:, :] = tail.astype(bf16)


def unpack(packed, cols, chips):
    count, crossed = blocks_of(cols)
    top, _ = packed_rows(cols, chips)
    half = LANES // 2
    row, col = grid_of(LANES, LANES)
    tail = packed[top:, :]
    grid = [[None] * count for _ in range(count)]
    at = 0
    for i, j in crossed:
        grid[i][j] = packed[at : at + LANES, :]
        grid[j][i] = grid[i][j].T
        at += LANES
    for i in range(0, count - 1, 2):
        mixed = packed[at : at + LANES, :]
        turned = mixed.T
        grid[i][i] = jnp.where(col >= row, mixed, turned)
        other = jnp.where(col < row, mixed, turned)
        grid[i + 1][i + 1] = jnp.where(col == row, tail[i + 1 : i + 2, :], other)
        at += LANES
    if count % 2:
        i = count - 1
        mixed = packed[at : at + half, :].astype(f32)
        turned = jnp.concatenate([mixed, mixed], axis=0).T
        r, c = row[:half], col[:half]
        upper = jnp.where(c >= r, mixed, turned[:half, :])
        corner = pltpu.roll(jnp.where(c < r, mixed, turned[:half, :]), half, 1)
        corner = jnp.where(c == r + half, tail[i : i + 1, :].astype(f32), corner)
        lower = jnp.where(c < half, turned[half:, :], corner)
        grid[i][i] = jnp.concatenate([upper, lower], axis=0).astype(bf16)
    gram = jnp.concatenate([jnp.concatenate(line, axis=1) for line in grid], axis=0)
    trace = jnp.sum(tail[count : count + 2 * chips, :].astype(f32), keepdims=True)
    return gram, trace


def symmetric_dot(p, q):
    wide = p.shape[0] - LANES
    left = jnp.dot(p, q[:, :wide], preferred_element_type=f32)
    corner = jnp.dot(p[wide:], q[:, wide:], preferred_element_type=f32)
    right = [left[wide:, i * LANES : (i + 1) * LANES].T for i in range(wide // LANES)] + [corner]
    return jnp.concatenate([left, jnp.concatenate(right, axis=0)], axis=1)


def writes(blocks, core, out_ref, sem):
    copies = []
    for ref, slots, other in blocks:
        which = 1 - core if other else core
        for k, (base, step) in enumerate(slots):
            copies.append(
                pltpu.make_async_copy(ref.at[k], out_ref.at[0, base + step * which], sem.at[len(copies)])
            )
    return copies


def update_kernel(chips, rows, slots, places, place_ref, counts_ref, *refs):
    n = len(slots)
    mine, told, kept, got = (refs[i * n : (i + 1) * n] for i in range(4))
    out_ref, back_ref = refs[4 * n :]
    _, strip, cols = kept[0].shape
    core, inner, own_count = place_ref[0], place_ref[2], counts_ref[0]
    a, b, c = poly_first, poly_second, poly_third
    dot = functools.partial(jnp.dot, preferred_element_type=f32)
    span = range(n)
    gram, scale = [], []
    for k in span:
        full, trace = unpack(jnp.where(inner == 1, mine[k][...], told[k][...]), cols, chips)
        gram.append(full)
        scale.append(1.0 / (jnp.sqrt(trace) + 1e-07))
    square = [v * v for v in scale]
    product = [symmetric_dot(g, g) for g in gram]
    poly = [
        ((b * square[k]) * gram[k].astype(f32) + (c * square[k] * square[k]) * product[k]).astype(bf16)
        for k in span
    ]
    x = [jnp.concatenate([kept[k][places[k]], got[k][places[k]]], axis=0) for k in span]
    once = [square[k] * symmetric_dot(poly[k], gram[k]) for k in span]
    current = [(a * x[k].astype(f32) + dot(x[k], poly[k])).astype(bf16) for k in span]
    twice = [symmetric_dot(poly[k], once[k].astype(bf16)) for k in span]
    second = [
        ((a * a * square[k]) * gram[k].astype(f32) + (2.0 * a) * once[k] + twice[k]).astype(bf16)
        for k in span
    ]
    cubic = [dot(current[k], second[k]) for k in span]
    fifth = [dot(cubic[k].astype(bf16), second[k]) for k in span]
    for k in span:
        out = a * current[k].astype(f32) + b * cubic[k] + c * fifth[k]
        live = slots[k][0] + core * slots[k][1] < own_count
        out = jnp.where(live, (math.sqrt(rows) * scale[k]) * out, 0.0).astype(bf16)
        out_ref[k] = out[:strip]
        back_ref[k] = out[strip:]


def join_kernel(ready, place_ref, *refs):
    blocks = [(ref, *block) for ref, block in zip(refs, ready)]
    copies = writes(blocks, place_ref[0], *refs[-2:])
    for copy in copies:
        copy.start()
    for copy in copies:
        copy.wait()


SMEM = pl.BlockSpec(memory_space=pltpu.SMEM)
VMEM = pl.BlockSpec(memory_space=pltpu.VMEM)
ANY = pl.BlockSpec(memory_space=pl.ANY)
HBM = pl.BlockSpec(memory_space=pltpu.HBM)
PARAMS = pltpu.CompilerParams(vmem_limit_bytes=VMEM_LIMIT)


SLOTS = 16
CHUNKS = ((4, 1), (6, 1), (2, 1), (0, 1), (8, 1), (10, 1))
PASSED = {2: (13, -1), 3: (15, -1)}
GROUPS = ((0, -2), (1, 2, -3, 3), (4, 5))
CALLS = ((0, 1, 2, 3), (-2, 4, -3, 5))
LAG = 4


def slot_of(k):
    return CHUNKS[k] if k >= 0 else PASSED[-k]


def sum_grams(grads, counts):
    held = grads[0]
    slots, strip, cols = held.shape
    devices = lax.axis_size("dp")
    chips = devices // CORES
    position = lax.axis_index("dp")
    core, chip = position % CORES, position // CORES
    inner = (chip == 1) | (chip == 2)
    place = jnp.stack([core, chip, inner.astype(jnp.int32)]).astype(jnp.int32)
    _, total = packed_rows(cols, chips)
    chunks = len(CHUNKS)

    def along(pairs):
        return [(CORES * i + k, CORES * j + k) for i, j in pairs for k in range(CORES)]

    swap = [(i, i ^ 1) for i in range(devices)]
    beside = along([(0, 1), (1, 0), (2, 3), (3, 2)])
    across = along([(1, 2), (2, 1)]) + [(i, i ^ 1) for i in (0, 1, devices - 2, devices - 1)]
    partner = [(i, i ^ 1) for i in range(lax.axis_size("expert"))]

    def cost(flops, moved):
        return pl.CostEstimate(flops=int(flops), bytes_accessed=int(moved), transcendentals=0)

    groups = [[slot_of(k) for k in group] for group in GROUPS]
    piece = [jax.ShapeDtypeStruct((len(group), strip, cols), bf16) for group in groups]
    parts = pl.pallas_call(
        functools.partial(split_kernel, groups),
        out_shape=piece + piece,
        in_specs=[SMEM, HBM],
        out_specs=[VMEM] * (2 * len(groups)),
        scratch_shapes=[pltpu.SemaphoreType.DMA((slots,))],
        compiler_params=PARAMS,
        name="split",
    )(place, pltpu.with_memory_space_constraint(held, pltpu.HBM))
    kept, sent = parts[: len(groups)], parts[len(groups) :]
    got, gram, where = [], {}, {}
    for i, group in enumerate(groups):
        size = len(group)
        got.append(lax.ppermute(sent[i], "dp", swap))
        outs = pl.pallas_call(
            functools.partial(gram_kernel, chips, group),
            out_shape=[jax.ShapeDtypeStruct((total, LANES), bf16)] * size,
            in_specs=[SMEM, SMEM, VMEM, VMEM],
            out_specs=[VMEM] * size,
            compiler_params=PARAMS,
            cost_estimate=cost(4 * size * strip * cols * cols, 4 * size * strip * cols),
            name="gram",
        )(place, counts, kept[i], got[i])
        for k, name in enumerate(GROUPS[i]):
            gram[name], where[name] = outs[k], (i, k)
    for k in PASSED:
        came = lax.ppermute(gram[-k], "expert", partner)
        gram[k] = gram[k] + came

    def chosen(one, other):
        return lax.select(jnp.broadcast_to(inner, one.shape), one, other)

    full, told, half = {}, {}, {}
    for t in range(chunks + LAG):
        k = t - LAG
        if k >= 0:
            came = lax.ppermute(half[k], "dp", across)
            full[k] = half[k] + came
        if k < 0:
            load = gram[t]
        elif t < chunks:
            load = chosen(full[k], gram[t])
        else:
            load = full[k]
        came = lax.ppermute(load, "dp", beside)
        if t < chunks:
            half[t] = gram[t] + came
        if k >= 0:
            told[k] = came
    for k in PASSED:
        load = chosen(full[k], told[k])
        full[-k] = told[-k] = lax.ppermute(load, "expert", partner)

    calls = [[slot_of(k) for k in call] for call in CALLS]
    waiting = []
    for i, call in enumerate(CALLS):
        n = len(call)
        out = jax.ShapeDtypeStruct((n, strip, cols), bf16)
        outs = pl.pallas_call(
            functools.partial(
                update_kernel,
                chips,
                strip * devices,
                calls[i],
                [where[k][1] for k in call],
            ),
            out_shape=[out, out],
            in_specs=[SMEM, SMEM] + [VMEM] * (4 * n),
            out_specs=[VMEM, VMEM],
            compiler_params=PARAMS,
            cost_estimate=cost(8 * n * cols**3 + 8 * n * strip * cols * cols, 8 * n * strip * cols),
            name="update",
        )(
            place,
            counts,
            *[full[k] for k in call],
            *[told[k] for k in call],
            *[kept[where[k][0]] for k in call],
            *[got[where[k][0]] for k in call],
        )
        came = lax.ppermute(outs[1], "dp", swap)
        waiting += [(outs[0], calls[i], False), (came, calls[i], True)]
    return pl.pallas_call(
        functools.partial(join_kernel, [block[1:] for block in waiting]),
        out_shape=jax.ShapeDtypeStruct((1,) + held.shape, bf16),
        in_specs=[SMEM] + [VMEM] * len(waiting),
        out_specs=HBM,
        scratch_shapes=[pltpu.SemaphoreType.DMA((slots,))],
        compiler_params=PARAMS,
        name="join",
    )(place, *[block[0] for block in waiting])


def solution(mesh):
    placed = (P("expert", None, "dp", None), P("expert"))
    devices = mesh.shape["dp"]

    def step(grads, counts):
        _, slots, rows, cols = grads.shape
        strip = rows // devices
        summed = devices == 4 * CORES and cols % LANES == 0 and slots == SLOTS and mesh.shape["expert"] % 2 == 0
        summed = summed and CORES * strip * cols >= packed_rows(cols, devices // CORES)[1] * LANES

        def per_device(grads, counts):
            return (sum_grams if summed else strips_to_owners)(grads, counts)

        mapped = jax.shard_map(
            per_device,
            mesh=mesh,
            in_specs=placed,
            out_specs=P("expert", None, "dp", None),
            check_vma=False,
        )
        return mapped(grads, counts)

    return step
```

```python
import functools
import math

import jax
import jax.numpy as jnp
from jax import lax
from jax.experimental import pallas as pl
from jax.experimental.pallas import tpu as pltpu
from jax.sharding import PartitionSpec as P


NS_STEPS = 2


poly_first = 3.4445
poly_second = -4.775
poly_third = 2.0315

LANES = 128
CORES = 2
VMEM_LIMIT = 16 << 20

f32 = jnp.float32
bf16 = jnp.bfloat16


def from_partner(block, axis, apart):
    count = lax.axis_size(axis)
    route = []
    for low in range(count):
        high = low | 1 << apart
        if high != low and high < count:
            route += [(low, high), (high, low)]
    return lax.ppermute(block, axis, route)


def orthogonalize(matrix):
    values = matrix.astype(jnp.float32)
    frob_norm = jnp.sqrt(jnp.sum(values * values))
    current = (values / (frob_norm + 1e-07)).astype(jnp.bfloat16)
    scale_out = math.sqrt(matrix.shape[0])
    result = jnp.zeros_like(matrix)
    for iteration in range(NS_STEPS):
        gram_matrix = lax.dot_general(
            current, current, (((0,), (0,)), ((), ())), preferred_element_type=jnp.float32
        ).astype(jnp.bfloat16)
        squared = jnp.dot(gram_matrix, gram_matrix, preferred_element_type=jnp.float32)
        poly_matrix = (poly_second * gram_matrix.astype(jnp.float32) + poly_third * squared).astype(
            jnp.bfloat16
        )
        updated = poly_first * current.astype(jnp.float32) + jnp.dot(
            current, poly_matrix, preferred_element_type=jnp.float32
        )
        if iteration + 1 < NS_STEPS:
            current = updated.astype(jnp.bfloat16)
        else:
            result = (updated * scale_out).astype(jnp.bfloat16)
    return result


def blank(matrix):
    return jnp.zeros_like(matrix)


def strips_to_owners(grads, counts):
    held = grads[0]
    own_count = counts[0]
    total_slots = held.shape[0]
    half_slots = total_slots // 2
    position = lax.axis_index("dp")
    slot_ids = jnp.arange(half_slots, dtype=jnp.int32)
    received, partner_counts = from_partner((held[half_slots:], counts), "expert", 0)
    incoming = jnp.flip(received, 0)
    surplus_in = partner_counts[0] - half_slots
    keep_own = slot_ids < own_count
    balanced = jnp.where(keep_own[:, None, None], held[:half_slots], incoming)
    live_flags = keep_own | (slot_ids >= half_slots - surplus_in)
    gathered = lax.all_to_all(balanced, "dp", split_axis=0, concat_axis=1, tiled=True)
    finished = lax.cond(live_flags[position], orthogonalize, blank, gathered[0])[None]
    restored = lax.all_to_all(finished, "dp", split_axis=1, concat_axis=0, tiled=True)
    returned = from_partner(restored, "expert", 0)
    lower_part = jnp.where(keep_own[:, None, None], restored, jnp.zeros_like(restored))
    upper_keep = slot_ids + half_slots < own_count
    upper_part = jnp.where(
        upper_keep[:, None, None], jnp.flip(returned, 0), jnp.zeros_like(returned)
    )
    result = jnp.concatenate([lower_part, upper_part], axis=0)
    return result[None]


def blocks_of(cols):
    count = cols // LANES
    crossed = [(i, j) for i in range(count) for j in range(i + 1, count)]
    return count, crossed


def packed_rows(cols, chips):
    count, crossed = blocks_of(cols)
    rows = LANES * (len(crossed) + count // 2) + (LANES // 2) * (count % 2)
    spare = -(-(count + 2 * chips) // 16) * 16
    return rows, rows + spare


def grid_of(rows, cols):
    return (
        lax.broadcasted_iota(jnp.int32, (rows, cols), 0),
        lax.broadcasted_iota(jnp.int32, (rows, cols), 1),
    )


def split_kernel(groups, place_ref, held_ref, *refs):
    n = len(groups)
    kept, sent, sem = refs[:n], refs[n : 2 * n], refs[2 * n]
    core = place_ref[0]
    copies = []
    for i, group in enumerate(groups):
        for ref, which in ((sent[i], 1 - core), (kept[i], core)):
            for k, (base, step) in enumerate(group):
                copies.append(
                    pltpu.make_async_copy(held_ref.at[base + step * which], ref.at[k], sem.at[len(copies)])
                )
    for copy in copies:
        copy.start()
    for copy in copies:
        copy.wait()


def gram_kernel(chips, group, place_ref, counts_ref, kept_ref, got_ref, *out_refs):
    size, _, cols = kept_ref.shape
    count, crossed = blocks_of(cols)
    top, total = packed_rows(cols, chips)
    half = LANES // 2
    row, col = grid_of(LANES, LANES)
    line, _ = grid_of(total - top, LANES)
    chip = place_ref[1]
    for s in range(size):
        x = jnp.concatenate([kept_ref[s], got_ref[s]], axis=0)
        base, step = group[s]
        live = base + step * place_ref[0] < counts_ref[0]
        x = jnp.where(live, x, jnp.zeros_like(x))
        g = lax.dot_general(x, x, (((0,), (0,)), ((), ())), preferred_element_type=f32)

        def block(i, j):
            return g[i * LANES : (i + 1) * LANES, j * LANES : (j + 1) * LANES]

        at = 0
        for i, j in crossed:
            out_refs[s][at : at + LANES, :] = block(i, j).astype(bf16)
            at += LANES
        diagonals = [
            jnp.sum(jnp.where(row == col, block(i, i), 0.0), axis=0, keepdims=True)
            for i in range(count)
        ]
        for i in range(0, count - 1, 2):
            mixed = jnp.where(col >= row, block(i, i), block(i + 1, i + 1))
            out_refs[s][at : at + LANES, :] = mixed.astype(bf16)
            at += LANES
        if count % 2:
            last = block(count - 1, count - 1)
            turned = pltpu.roll(last[half:, :], half, 1)
            mixed = jnp.where(col[:half] >= row[:half], last[:half, :], turned)
            out_refs[s][at : at + half, :] = mixed.astype(bf16)
            at += half
        tail = jnp.zeros((total - top, LANES), f32)
        for i in range(count):
            tail = jnp.where(line == i, diagonals[i], tail)
        trace = sum(diagonals)
        coarse = trace.astype(bf16).astype(f32)
        tail = jnp.where(line == count + 2 * chip, coarse, tail)
        tail = jnp.where(line == count + 2 * chip + 1, trace - coarse, tail)
        out_refs[s][top:, :] = tail.astype(bf16)


def unpack(packed, cols, chips):
    count, crossed = blocks_of(cols)
    top, _ = packed_rows(cols, chips)
    half = LANES // 2
    row, col = grid_of(LANES, LANES)
    tail = packed[top:, :]
    grid = [[None] * count for _ in range(count)]
    at = 0
    for i, j in crossed:
        grid[i][j] = packed[at : at + LANES, :]
        grid[j][i] = grid[i][j].T
        at += LANES
    for i in range(0, count - 1, 2):
        mixed = packed[at : at + LANES, :]
        turned = mixed.T
        grid[i][i] = jnp.where(col >= row, mixed, turned)
        other = jnp.where(col < row, mixed, turned)
        grid[i + 1][i + 1] = jnp.where(col == row, tail[i + 1 : i + 2, :], other)
        at += LANES
    if count % 2:
        i = count - 1
        mixed = packed[at : at + half, :].astype(f32)
        turned = jnp.concatenate([mixed, mixed], axis=0).T
        r, c = row[:half], col[:half]
        upper = jnp.where(c >= r, mixed, turned[:half, :])
        corner = pltpu.roll(jnp.where(c < r, mixed, turned[:half, :]), half, 1)
        corner = jnp.where(c == r + half, tail[i : i + 1, :].astype(f32), corner)
        lower = jnp.where(c < half, turned[half:, :], corner)
        grid[i][i] = jnp.concatenate([upper, lower], axis=0).astype(bf16)
    gram = jnp.concatenate([jnp.concatenate(line, axis=1) for line in grid], axis=0)
    trace = jnp.sum(tail[count : count + 2 * chips, :].astype(f32), keepdims=True)
    return gram, trace


def parts_of(matrix):
    wide = matrix.shape[0] - LANES
    return matrix[:, :wide], matrix[wide:, wide:]


def symmetric_dot(p, q):
    wide = p.shape[0] - LANES
    left = jnp.dot(p, q[:, :wide], preferred_element_type=f32)
    corner = jnp.dot(p[wide:], q[:, wide:], preferred_element_type=f32)
    return left, corner


def completed(parts):
    left, corner = (part.astype(bf16) for part in parts)
    wide = left.shape[1]
    right = [left[wide:, i * LANES : (i + 1) * LANES].T for i in range(wide // LANES)] + [corner]
    return jnp.concatenate([left, jnp.concatenate(right, axis=0)], axis=1)


def writes(blocks, core, out_ref, sem):
    copies = []
    for ref, slots, other in blocks:
        which = 1 - core if other else core
        for k, (base, step) in enumerate(slots):
            copies.append(
                pltpu.make_async_copy(ref.at[k], out_ref.at[0, base + step * which], sem.at[len(copies)])
            )
    return copies


def update_kernel(chips, rows, slots, places, place_ref, counts_ref, *refs):
    n = len(slots)
    mine, told, kept, got = (refs[i * n : (i + 1) * n] for i in range(4))
    out_ref, back_ref = refs[4 * n :]
    _, strip, cols = kept[0].shape
    core, inner, own_count = place_ref[0], place_ref[2], counts_ref[0]
    a, b, c = poly_first, poly_second, poly_third
    dot = functools.partial(jnp.dot, preferred_element_type=f32)
    span = range(n)
    gram, scale = [], []
    for k in span:
        full, trace = unpack(jnp.where(inner == 1, mine[k][...], told[k][...]), cols, chips)
        gram.append(full)
        scale.append(1.0 / (jnp.sqrt(trace) + 1e-07))
    square = [v * v for v in scale]
    half = range(2)
    first = [[part.astype(f32) for part in parts_of(g)] for g in gram]
    product = [symmetric_dot(g, g) for g in gram]
    poly = [
        completed(
            [(b * square[k]) * first[k][i] + (c * square[k] * square[k]) * product[k][i] for i in half]
        )
        for k in span
    ]
    x = [jnp.concatenate([kept[k][places[k]], got[k][places[k]]], axis=0) for k in span]
    once = [[square[k] * part for part in symmetric_dot(poly[k], gram[k])] for k in span]
    current = [(a * x[k].astype(f32) + dot(x[k], poly[k])).astype(bf16) for k in span]
    twice = [symmetric_dot(poly[k], completed(once[k])) for k in span]
    second = [
        completed(
            [
                (a * a * square[k]) * first[k][i] + (2.0 * a) * once[k][i] + twice[k][i]
                for i in half
            ]
        )
        for k in span
    ]
    cubic = [dot(current[k], second[k]) for k in span]
    fifth = [dot(cubic[k].astype(bf16), second[k]) for k in span]
    for k in span:
        out = a * current[k].astype(f32) + b * cubic[k] + c * fifth[k]
        live = slots[k][0] + core * slots[k][1] < own_count
        out = jnp.where(live, (math.sqrt(rows) * scale[k]) * out, 0.0).astype(bf16)
        out_ref[k] = out[:strip]
        back_ref[k] = out[strip:]


def join_kernel(ready, place_ref, *refs):
    blocks = [(ref, *block) for ref, block in zip(refs, ready)]
    copies = writes(blocks, place_ref[0], *refs[-2:])
    for copy in copies:
        copy.start()
    for copy in copies:
        copy.wait()


SMEM = pl.BlockSpec(memory_space=pltpu.SMEM)
VMEM = pl.BlockSpec(memory_space=pltpu.VMEM)
ANY = pl.BlockSpec(memory_space=pl.ANY)
HBM = pl.BlockSpec(memory_space=pltpu.HBM)
PARAMS = pltpu.CompilerParams(vmem_limit_bytes=VMEM_LIMIT)


SLOTS = 16
CHUNKS = ((4, 1), (6, 1), (2, 1), (0, 1), (8, 1), (10, 1))
PASSED = {2: (13, -1), 3: (15, -1)}
GROUPS = ((0, -2), (1, 2, -3, 3, 4, 5))
CALLS = ((0, 1, 2, 3), (-2, 4, -3, 5))
LAG = 4


def slot_of(k):
    return CHUNKS[k] if k >= 0 else PASSED[-k]


def sum_grams(grads, counts):
    held = grads[0]
    slots, strip, cols = held.shape
    devices = lax.axis_size("dp")
    chips = devices // CORES
    position = lax.axis_index("dp")
    core, chip = position % CORES, position // CORES
    inner = (chip == 1) | (chip == 2)
    place = jnp.stack([core, chip, inner.astype(jnp.int32)]).astype(jnp.int32)
    _, total = packed_rows(cols, chips)
    chunks = len(CHUNKS)

    def along(pairs):
        return [(CORES * i + k, CORES * j + k) for i, j in pairs for k in range(CORES)]

    swap = [(i, i ^ 1) for i in range(devices)]
    beside = along([(0, 1), (1, 0), (2, 3), (3, 2)])
    across = along([(1, 2), (2, 1)]) + [(i, i ^ 1) for i in (0, 1, devices - 2, devices - 1)]
    partner = [(i, i ^ 1) for i in range(lax.axis_size("expert"))]

    def cost(flops, moved):
        return pl.CostEstimate(flops=int(flops), bytes_accessed=int(moved), transcendentals=0)

    groups = [[slot_of(k) for k in group] for group in GROUPS]
    piece = [jax.ShapeDtypeStruct((len(group), strip, cols), bf16) for group in groups]
    parts = pl.pallas_call(
        functools.partial(split_kernel, groups),
        out_shape=piece + piece,
        in_specs=[SMEM, HBM],
        out_specs=[VMEM] * (2 * len(groups)),
        scratch_shapes=[pltpu.SemaphoreType.DMA((slots,))],
        compiler_params=PARAMS,
        name="split",
    )(place, pltpu.with_memory_space_constraint(held, pltpu.HBM))
    kept, sent = parts[: len(groups)], parts[len(groups) :]
    got, gram, where = [], {}, {}
    for i, group in enumerate(groups):
        size = len(group)
        got.append(lax.ppermute(sent[i], "dp", swap))
        outs = pl.pallas_call(
            functools.partial(gram_kernel, chips, group),
            out_shape=[jax.ShapeDtypeStruct((total, LANES), bf16)] * size,
            in_specs=[SMEM, SMEM, VMEM, VMEM],
            out_specs=[VMEM] * size,
            compiler_params=PARAMS,
            cost_estimate=cost(4 * size * strip * cols * cols, 4 * size * strip * cols),
            name="gram",
        )(place, counts, kept[i], got[i])
        for k, name in enumerate(GROUPS[i]):
            gram[name], where[name] = outs[k], (i, k)
    for k in PASSED:
        came = lax.ppermute(gram[-k], "expert", partner)
        gram[k] = gram[k] + came

    def chosen(one, other):
        return lax.select(jnp.broadcast_to(inner, one.shape), one, other)

    full, told, half = {}, {}, {}
    for t in range(chunks + LAG):
        k = t - LAG
        if k >= 0:
            came = lax.ppermute(half[k], "dp", across)
            full[k] = half[k] + came
        if k < 0:
            load = gram[t]
        elif t < chunks:
            load = chosen(full[k], gram[t])
        else:
            load = full[k]
        came = lax.ppermute(load, "dp", beside)
        if t < chunks:
            half[t] = gram[t] + came
        if k >= 0:
            told[k] = came
    for k in PASSED:
        load = chosen(full[k], told[k])
        full[-k] = told[-k] = lax.ppermute(load, "expert", partner)

    calls = [[slot_of(k) for k in call] for call in CALLS]
    waiting = []
    for i, call in enumerate(CALLS):
        n = len(call)
        out = jax.ShapeDtypeStruct((n, strip, cols), bf16)
        outs = pl.pallas_call(
            functools.partial(
                update_kernel,
                chips,
                strip * devices,
                calls[i],
                [where[k][1] for k in call],
            ),
            out_shape=[out, out],
            in_specs=[SMEM, SMEM] + [VMEM] * (4 * n),
            out_specs=[VMEM, VMEM],
            compiler_params=PARAMS,
            cost_estimate=cost(8 * n * cols**3 + 8 * n * strip * cols * cols, 8 * n * strip * cols),
            name="update",
        )(
            place,
            counts,
            *[full[k] for k in call],
            *[told[k] for k in call],
            *[kept[where[k][0]] for k in call],
            *[got[where[k][0]] for k in call],
        )
        came = lax.ppermute(outs[1], "dp", swap)
        waiting += [(outs[0], calls[i], False), (came, calls[i], True)]
    return pl.pallas_call(
        functools.partial(join_kernel, [block[1:] for block in waiting]),
        out_shape=jax.ShapeDtypeStruct((1,) + held.shape, bf16),
        in_specs=[SMEM] + [VMEM] * len(waiting),
        out_specs=HBM,
        scratch_shapes=[pltpu.SemaphoreType.DMA((slots,))],
        compiler_params=PARAMS,
        name="join",
    )(place, *[block[0] for block in waiting])


def solution(mesh):
    placed = (P("expert", None, "dp", None), P("expert"))
    devices = mesh.shape["dp"]

    def step(grads, counts):
        _, slots, rows, cols = grads.shape
        strip = rows // devices
        summed = devices == 4 * CORES and cols % LANES == 0 and slots == SLOTS and mesh.shape["expert"] % 2 == 0
        summed = summed and CORES * strip * cols >= packed_rows(cols, devices // CORES)[1] * LANES

        def per_device(grads, counts):
            return (sum_grams if summed else strips_to_owners)(grads, counts)

        mapped = jax.shard_map(
            per_device,
            mesh=mesh,
            in_specs=placed,
            out_specs=P("expert", None, "dp", None),
            check_vma=False,
        )
        return mapped(grads, counts)

    return step
```

```python
import functools
import math

import jax
import jax.numpy as jnp
from jax import lax
from jax.experimental import pallas as pl
from jax.experimental.pallas import tpu as pltpu
from jax.sharding import PartitionSpec as P


NS_STEPS = 2


poly_first = 3.4445
poly_second = -4.775
poly_third = 2.0315

LANES = 128
CORES = 2
VMEM_LIMIT = 16 << 20

f32 = jnp.float32
bf16 = jnp.bfloat16


def from_partner(block, axis, apart):
    count = lax.axis_size(axis)
    route = []
    for low in range(count):
        high = low | 1 << apart
        if high != low and high < count:
            route += [(low, high), (high, low)]
    return lax.ppermute(block, axis, route)


def orthogonalize(matrix):
    values = matrix.astype(jnp.float32)
    frob_norm = jnp.sqrt(jnp.sum(values * values))
    current = (values / (frob_norm + 1e-07)).astype(jnp.bfloat16)
    scale_out = math.sqrt(matrix.shape[0])
    result = jnp.zeros_like(matrix)
    for iteration in range(NS_STEPS):
        gram_matrix = lax.dot_general(
            current, current, (((0,), (0,)), ((), ())), preferred_element_type=jnp.float32
        ).astype(jnp.bfloat16)
        squared = jnp.dot(gram_matrix, gram_matrix, preferred_element_type=jnp.float32)
        poly_matrix = (poly_second * gram_matrix.astype(jnp.float32) + poly_third * squared).astype(
            jnp.bfloat16
        )
        updated = poly_first * current.astype(jnp.float32) + jnp.dot(
            current, poly_matrix, preferred_element_type=jnp.float32
        )
        if iteration + 1 < NS_STEPS:
            current = updated.astype(jnp.bfloat16)
        else:
            result = (updated * scale_out).astype(jnp.bfloat16)
    return result


def blank(matrix):
    return jnp.zeros_like(matrix)


def strips_to_owners(grads, counts):
    held = grads[0]
    own_count = counts[0]
    total_slots = held.shape[0]
    half_slots = total_slots // 2
    position = lax.axis_index("dp")
    slot_ids = jnp.arange(half_slots, dtype=jnp.int32)
    received, partner_counts = from_partner((held[half_slots:], counts), "expert", 0)
    incoming = jnp.flip(received, 0)
    surplus_in = partner_counts[0] - half_slots
    keep_own = slot_ids < own_count
    balanced = jnp.where(keep_own[:, None, None], held[:half_slots], incoming)
    live_flags = keep_own | (slot_ids >= half_slots - surplus_in)
    gathered = lax.all_to_all(balanced, "dp", split_axis=0, concat_axis=1, tiled=True)
    finished = lax.cond(live_flags[position], orthogonalize, blank, gathered[0])[None]
    restored = lax.all_to_all(finished, "dp", split_axis=1, concat_axis=0, tiled=True)
    returned = from_partner(restored, "expert", 0)
    lower_part = jnp.where(keep_own[:, None, None], restored, jnp.zeros_like(restored))
    upper_keep = slot_ids + half_slots < own_count
    upper_part = jnp.where(
        upper_keep[:, None, None], jnp.flip(returned, 0), jnp.zeros_like(returned)
    )
    result = jnp.concatenate([lower_part, upper_part], axis=0)
    return result[None]


def blocks_of(cols):
    count = cols // LANES
    crossed = [(i, j) for i in range(count) for j in range(i + 1, count)]
    return count, crossed


def packed_rows(cols, chips):
    count, crossed = blocks_of(cols)
    rows = LANES * (len(crossed) + count // 2) + (LANES // 2) * (count % 2)
    spare = -(-(count + 2 * chips) // 16) * 16
    return rows, rows + spare


def grid_of(rows, cols):
    return (
        lax.broadcasted_iota(jnp.int32, (rows, cols), 0),
        lax.broadcasted_iota(jnp.int32, (rows, cols), 1),
    )


def split_kernel(groups, place_ref, held_ref, *refs):
    n = len(groups)
    kept, sent, sem = refs[:n], refs[n : 2 * n], refs[2 * n]
    core = place_ref[0]
    copies = []
    for i, group in enumerate(groups):
        for ref, which in ((sent[i], 1 - core), (kept[i], core)):
            for k, (base, step) in enumerate(group):
                copies.append(
                    pltpu.make_async_copy(held_ref.at[base + step * which], ref.at[k], sem.at[len(copies)])
                )
    for copy in copies:
        copy.start()
    for copy in copies:
        copy.wait()


def gram_kernel(chips, group, place_ref, counts_ref, kept_ref, got_ref, *out_refs):
    size, _, cols = kept_ref.shape
    count, crossed = blocks_of(cols)
    top, total = packed_rows(cols, chips)
    half = LANES // 2
    row, col = grid_of(LANES, LANES)
    line, _ = grid_of(total - top, LANES)
    chip = place_ref[1]
    for s in range(size):
        x = jnp.concatenate([kept_ref[s], got_ref[s]], axis=0)
        base, step = group[s]
        live = base + step * place_ref[0] < counts_ref[0]
        x = jnp.where(live, x, jnp.zeros_like(x))
        g = lax.dot_general(x, x, (((0,), (0,)), ((), ())), preferred_element_type=f32)

        def block(i, j):
            return g[i * LANES : (i + 1) * LANES, j * LANES : (j + 1) * LANES]

        at = 0
        for i, j in crossed:
            out_refs[s][at : at + LANES, :] = block(i, j).astype(bf16)
            at += LANES
        diagonals = [
            jnp.sum(jnp.where(row == col, block(i, i), 0.0), axis=0, keepdims=True)
            for i in range(count)
        ]
        for i in range(0, count - 1, 2):
            mixed = jnp.where(col >= row, block(i, i), block(i + 1, i + 1))
            out_refs[s][at : at + LANES, :] = mixed.astype(bf16)
            at += LANES
        if count % 2:
            last = block(count - 1, count - 1)
            turned = pltpu.roll(last[half:, :], half, 1)
            mixed = jnp.where(col[:half] >= row[:half], last[:half, :], turned)
            out_refs[s][at : at + half, :] = mixed.astype(bf16)
            at += half
        tail = jnp.zeros((total - top, LANES), f32)
        for i in range(count):
            tail = jnp.where(line == i, diagonals[i], tail)
        trace = sum(diagonals)
        coarse = trace.astype(bf16).astype(f32)
        tail = jnp.where(line == count + 2 * chip, coarse, tail)
        tail = jnp.where(line == count + 2 * chip + 1, trace - coarse, tail)
        out_refs[s][top:, :] = tail.astype(bf16)


def unpack(packed, cols, chips):
    count, crossed = blocks_of(cols)
    top, _ = packed_rows(cols, chips)
    half = LANES // 2
    row, col = grid_of(LANES, LANES)
    tail = packed[top:, :]
    grid = [[None] * count for _ in range(count)]
    at = 0
    for i, j in crossed:
        grid[i][j] = packed[at : at + LANES, :]
        grid[j][i] = grid[i][j].T
        at += LANES
    for i in range(0, count - 1, 2):
        mixed = packed[at : at + LANES, :]
        turned = mixed.T
        grid[i][i] = jnp.where(col >= row, mixed, turned)
        other = jnp.where(col < row, mixed, turned)
        grid[i + 1][i + 1] = jnp.where(col == row, tail[i + 1 : i + 2, :], other)
        at += LANES
    if count % 2:
        i = count - 1
        mixed = packed[at : at + half, :].astype(f32)
        turned = jnp.concatenate([mixed, mixed], axis=0).T
        r, c = row[:half], col[:half]
        upper = jnp.where(c >= r, mixed, turned[:half, :])
        corner = pltpu.roll(jnp.where(c < r, mixed, turned[:half, :]), half, 1)
        corner = jnp.where(c == r + half, tail[i : i + 1, :].astype(f32), corner)
        lower = jnp.where(c < half, turned[half:, :], corner)
        grid[i][i] = jnp.concatenate([upper, lower], axis=0).astype(bf16)
    gram = jnp.concatenate([jnp.concatenate(line, axis=1) for line in grid], axis=0)
    trace = jnp.sum(tail[count : count + 2 * chips, :].astype(f32), keepdims=True)
    return gram, trace


def parts_of(matrix):
    wide = matrix.shape[0] - LANES
    return matrix[:, :wide], matrix[wide:, wide:]


def symmetric_dot(p, q):
    wide = p.shape[0] - LANES
    left = jnp.dot(p, q[:, :wide], preferred_element_type=f32)
    corner = jnp.dot(p[wide:], q[:, wide:], preferred_element_type=f32)
    return left, corner


def completed(parts):
    left, corner = (part.astype(bf16) for part in parts)
    wide = left.shape[1]
    right = [left[wide:, i * LANES : (i + 1) * LANES].T for i in range(wide // LANES)] + [corner]
    return jnp.concatenate([left, jnp.concatenate(right, axis=0)], axis=1)


def writes(blocks, core, out_ref, sem):
    copies = []
    for ref, slots, other in blocks:
        which = 1 - core if other else core
        for k, (base, step) in enumerate(slots):
            copies.append(
                pltpu.make_async_copy(ref.at[k], out_ref.at[0, base + step * which], sem.at[len(copies)])
            )
    return copies


def update_kernel(chips, rows, slots, places, place_ref, counts_ref, *refs):
    n = len(slots)
    mine, told, kept, got = (refs[i * n : (i + 1) * n] for i in range(4))
    out_ref, back_ref = refs[4 * n :]
    _, strip, cols = kept[0].shape
    core, inner, own_count = place_ref[0], place_ref[2], counts_ref[0]
    a, b, c = poly_first, poly_second, poly_third
    dot = functools.partial(jnp.dot, preferred_element_type=f32)
    span = range(n)
    gram, scale = [], []
    for k in span:
        full, trace = unpack(jnp.where(inner == 1, mine[k][...], told[k][...]), cols, chips)
        gram.append(full)
        scale.append(1.0 / (jnp.sqrt(trace) + 1e-07))
    square = [v * v for v in scale]
    half = range(2)
    first = [[part.astype(f32) for part in parts_of(g)] for g in gram]
    product = [symmetric_dot(g, g) for g in gram]
    poly = [
        completed(
            [(b * square[k]) * first[k][i] + (c * square[k] * square[k]) * product[k][i] for i in half]
        )
        for k in span
    ]
    x = [jnp.concatenate([kept[k][places[k]], got[k][places[k]]], axis=0).T for k in span]
    once = [[square[k] * part for part in symmetric_dot(poly[k], gram[k])] for k in span]
    current = [(a * x[k].astype(f32) + dot(poly[k], x[k])).astype(bf16) for k in span]
    twice = [symmetric_dot(poly[k], completed(once[k])) for k in span]
    second = [
        completed(
            [
                (a * a * square[k]) * first[k][i] + (2.0 * a) * once[k][i] + twice[k][i]
                for i in half
            ]
        )
        for k in span
    ]
    cubic = [dot(second[k], current[k]) for k in span]
    fifth = [dot(second[k], cubic[k].astype(bf16)) for k in span]
    for k in span:
        out = a * current[k].astype(f32) + b * cubic[k] + c * fifth[k]
        live = slots[k][0] + core * slots[k][1] < own_count
        out = jnp.where(live, (math.sqrt(rows) * scale[k]) * out, 0.0).astype(bf16).T
        out_ref[k] = out[:strip]
        back_ref[k] = out[strip:]


def join_kernel(ready, place_ref, *refs):
    blocks = [(ref, *block) for ref, block in zip(refs, ready)]
    copies = writes(blocks, place_ref[0], *refs[-2:])
    for copy in copies:
        copy.start()
    for copy in copies:
        copy.wait()


SMEM = pl.BlockSpec(memory_space=pltpu.SMEM)
VMEM = pl.BlockSpec(memory_space=pltpu.VMEM)
ANY = pl.BlockSpec(memory_space=pl.ANY)
HBM = pl.BlockSpec(memory_space=pltpu.HBM)
PARAMS = pltpu.CompilerParams(vmem_limit_bytes=VMEM_LIMIT)
UPDATE_PARAMS = pltpu.CompilerParams(vmem_limit_bytes=VMEM_LIMIT)


SLOTS = 16
CHUNKS = ((4, 1), (6, 1), (2, 1), (0, 1), (8, 1), (10, 1))
PASSED = {2: (13, -1), 3: (15, -1)}
GROUPS = ((0, -2), (1, 2, -3, 3), (4, 5))
CALLS = ((0, 1, 2, 3), (-2, 4, -3, 5))
LAG = 4


def slot_of(k):
    return CHUNKS[k] if k >= 0 else PASSED[-k]


def sum_grams(grads, counts):
    held = grads[0]
    slots, strip, cols = held.shape
    devices = lax.axis_size("dp")
    chips = devices // CORES
    position = lax.axis_index("dp")
    core, chip = position % CORES, position // CORES
    inner = (chip == 1) | (chip == 2)
    place = jnp.stack([core, chip, inner.astype(jnp.int32)]).astype(jnp.int32)
    _, total = packed_rows(cols, chips)
    chunks = len(CHUNKS)

    def along(pairs):
        return [(CORES * i + k, CORES * j + k) for i, j in pairs for k in range(CORES)]

    swap = [(i, i ^ 1) for i in range(devices)]
    beside = along([(0, 1), (1, 0), (2, 3), (3, 2)])
    across = along([(1, 2), (2, 1)]) + [(i, i ^ 1) for i in (0, 1, devices - 2, devices - 1)]
    partner = [(i, i ^ 1) for i in range(lax.axis_size("expert"))]

    def cost(flops, moved):
        return pl.CostEstimate(flops=int(flops), bytes_accessed=int(moved), transcendentals=0)

    groups = [[slot_of(k) for k in group] for group in GROUPS]
    piece = [jax.ShapeDtypeStruct((len(group), strip, cols), bf16) for group in groups]
    parts = pl.pallas_call(
        functools.partial(split_kernel, groups),
        out_shape=piece + piece,
        in_specs=[SMEM, HBM],
        out_specs=[VMEM] * (2 * len(groups)),
        scratch_shapes=[pltpu.SemaphoreType.DMA((slots,))],
        compiler_params=PARAMS,
        name="split",
    )(place, pltpu.with_memory_space_constraint(held, pltpu.HBM))
    kept, sent = parts[: len(groups)], parts[len(groups) :]
    got, gram, where = [], {}, {}
    for i, group in enumerate(groups):
        size = len(group)
        got.append(lax.ppermute(sent[i], "dp", swap))
        outs = pl.pallas_call(
            functools.partial(gram_kernel, chips, group),
            out_shape=[jax.ShapeDtypeStruct((total, LANES), bf16)] * size,
            in_specs=[SMEM, SMEM, VMEM, VMEM],
            out_specs=[VMEM] * size,
            compiler_params=PARAMS,
            cost_estimate=cost(4 * size * strip * cols * cols, 4 * size * strip * cols),
            name="gram",
        )(place, counts, kept[i], got[i])
        for k, name in enumerate(GROUPS[i]):
            gram[name], where[name] = outs[k], (i, k)
    for k in PASSED:
        came = lax.ppermute(gram[-k], "expert", partner)
        gram[k] = gram[k] + came

    def chosen(one, other):
        return lax.select(jnp.broadcast_to(inner, one.shape), one, other)

    full, told, half = {}, {}, {}
    for t in range(chunks + LAG):
        k = t - LAG
        if k >= 0:
            came = lax.ppermute(half[k], "dp", across)
            full[k] = half[k] + came
        if k < 0:
            load = gram[t]
        elif t < chunks:
            load = chosen(full[k], gram[t])
        else:
            load = full[k]
        came = lax.ppermute(load, "dp", beside)
        if t < chunks:
            half[t] = gram[t] + came
        if k >= 0:
            told[k] = came
    for k in PASSED:
        load = chosen(full[k], told[k])
        full[-k] = told[-k] = lax.ppermute(load, "expert", partner)

    calls = [[slot_of(k) for k in call] for call in CALLS]
    waiting = []
    for i, call in enumerate(CALLS):
        n = len(call)
        out = jax.ShapeDtypeStruct((n, strip, cols), bf16)
        outs = pl.pallas_call(
            functools.partial(
                update_kernel,
                chips,
                strip * devices,
                calls[i],
                [where[k][1] for k in call],
            ),
            out_shape=[out, out],
            in_specs=[SMEM, SMEM] + [VMEM] * (4 * n),
            out_specs=[VMEM, VMEM],
            compiler_params=UPDATE_PARAMS,
            cost_estimate=cost(8 * n * cols**3 + 8 * n * strip * cols * cols, 8 * n * strip * cols),
            name="update",
        )(
            place,
            counts,
            *[full[k] for k in call],
            *[told[k] for k in call],
            *[kept[where[k][0]] for k in call],
            *[got[where[k][0]] for k in call],
        )
        came = lax.ppermute(outs[1], "dp", swap)
        waiting += [(outs[0], calls[i], False), (came, calls[i], True)]
    return pl.pallas_call(
        functools.partial(join_kernel, [block[1:] for block in waiting]),
        out_shape=jax.ShapeDtypeStruct((1,) + held.shape, bf16),
        in_specs=[SMEM] + [VMEM] * len(waiting),
        out_specs=HBM,
        scratch_shapes=[pltpu.SemaphoreType.DMA((slots,))],
        compiler_params=PARAMS,
        name="join",
    )(place, *[block[0] for block in waiting])


def solution(mesh):
    placed = (P("expert", None, "dp", None), P("expert"))
    devices = mesh.shape["dp"]

    def step(grads, counts):
        _, slots, rows, cols = grads.shape
        strip = rows // devices
        summed = devices == 4 * CORES and cols % LANES == 0 and slots == SLOTS and mesh.shape["expert"] % 2 == 0
        summed = summed and CORES * strip * cols >= packed_rows(cols, devices // CORES)[1] * LANES

        def per_device(grads, counts):
            return (sum_grams if summed else strips_to_owners)(grads, counts)

        mapped = jax.shard_map(
            per_device,
            mesh=mesh,
            in_specs=placed,
            out_specs=P("expert", None, "dp", None),
            check_vma=False,
        )
        return mapped(grads, counts)

    return step
```

```python
import functools
import math

import jax
import jax.numpy as jnp
from jax import lax
from jax.experimental import pallas as pl
from jax.experimental.pallas import tpu as pltpu
from jax.sharding import PartitionSpec as P


NS_STEPS = 2


poly_first = 3.4445
poly_second = -4.775
poly_third = 2.0315

LANES = 128
CORES = 2
VMEM_LIMIT = 16 << 20

f32 = jnp.float32
bf16 = jnp.bfloat16


def from_partner(block, axis, apart):
    count = lax.axis_size(axis)
    route = []
    for low in range(count):
        high = low | 1 << apart
        if high != low and high < count:
            route += [(low, high), (high, low)]
    return lax.ppermute(block, axis, route)


def orthogonalize(matrix):
    values = matrix.astype(jnp.float32)
    frob_norm = jnp.sqrt(jnp.sum(values * values))
    current = (values / (frob_norm + 1e-07)).astype(jnp.bfloat16)
    scale_out = math.sqrt(matrix.shape[0])
    result = jnp.zeros_like(matrix)
    for iteration in range(NS_STEPS):
        gram_matrix = lax.dot_general(
            current, current, (((0,), (0,)), ((), ())), preferred_element_type=jnp.float32
        ).astype(jnp.bfloat16)
        squared = jnp.dot(gram_matrix, gram_matrix, preferred_element_type=jnp.float32)
        poly_matrix = (poly_second * gram_matrix.astype(jnp.float32) + poly_third * squared).astype(
            jnp.bfloat16
        )
        updated = poly_first * current.astype(jnp.float32) + jnp.dot(
            current, poly_matrix, preferred_element_type=jnp.float32
        )
        if iteration + 1 < NS_STEPS:
            current = updated.astype(jnp.bfloat16)
        else:
            result = (updated * scale_out).astype(jnp.bfloat16)
    return result


def blank(matrix):
    return jnp.zeros_like(matrix)


def strips_to_owners(grads, counts):
    held = grads[0]
    own_count = counts[0]
    total_slots = held.shape[0]
    half_slots = total_slots // 2
    position = lax.axis_index("dp")
    slot_ids = jnp.arange(half_slots, dtype=jnp.int32)
    received, partner_counts = from_partner((held[half_slots:], counts), "expert", 0)
    incoming = jnp.flip(received, 0)
    surplus_in = partner_counts[0] - half_slots
    keep_own = slot_ids < own_count
    balanced = jnp.where(keep_own[:, None, None], held[:half_slots], incoming)
    live_flags = keep_own | (slot_ids >= half_slots - surplus_in)
    gathered = lax.all_to_all(balanced, "dp", split_axis=0, concat_axis=1, tiled=True)
    finished = lax.cond(live_flags[position], orthogonalize, blank, gathered[0])[None]
    restored = lax.all_to_all(finished, "dp", split_axis=1, concat_axis=0, tiled=True)
    returned = from_partner(restored, "expert", 0)
    lower_part = jnp.where(keep_own[:, None, None], restored, jnp.zeros_like(restored))
    upper_keep = slot_ids + half_slots < own_count
    upper_part = jnp.where(
        upper_keep[:, None, None], jnp.flip(returned, 0), jnp.zeros_like(returned)
    )
    result = jnp.concatenate([lower_part, upper_part], axis=0)
    return result[None]


def blocks_of(cols):
    count = cols // LANES
    crossed = [(i, j) for i in range(count) for j in range(i + 1, count)]
    return count, crossed


def packed_rows(cols, chips):
    count, crossed = blocks_of(cols)
    rows = LANES * (len(crossed) + count // 2) + (LANES // 2) * (count % 2)
    spare = -(-(count + 2 * chips) // 16) * 16
    return rows, rows + spare


def grid_of(rows, cols):
    return (
        lax.broadcasted_iota(jnp.int32, (rows, cols), 0),
        lax.broadcasted_iota(jnp.int32, (rows, cols), 1),
    )


def split_kernel(groups, place_ref, held_ref, *refs):
    sent, sem = refs[:-1], refs[-1]
    other = 1 - place_ref[0]
    copies = []
    for ref, group in zip(sent, groups):
        for k, (base, step) in enumerate(group):
            copies.append(
                pltpu.make_async_copy(held_ref.at[base + step * other], ref.at[k], sem.at[len(copies)])
            )
    for copy in copies:
        copy.start()
    for copy in copies:
        copy.wait()


def gram_kernel(chips, group, place_ref, counts_ref, held_ref, got_ref, *out_refs):
    size, _, cols = got_ref.shape
    count, crossed = blocks_of(cols)
    top, total = packed_rows(cols, chips)
    half = LANES // 2
    row, col = grid_of(LANES, LANES)
    line, _ = grid_of(total - top, LANES)
    chip = place_ref[1]
    for s in range(size):
        base, step = group[s]
        x = jnp.concatenate([held_ref[base + step * place_ref[0]], got_ref[s]], axis=0)
        live = base + step * place_ref[0] < counts_ref[0]
        x = jnp.where(live, x, jnp.zeros_like(x))
        g = lax.dot_general(x, x, (((0,), (0,)), ((), ())), preferred_element_type=f32)

        def block(i, j):
            return g[i * LANES : (i + 1) * LANES, j * LANES : (j + 1) * LANES]

        at = 0
        for i, j in crossed:
            out_refs[s][at : at + LANES, :] = block(i, j).astype(bf16)
            at += LANES
        diagonals = [
            jnp.sum(jnp.where(row == col, block(i, i), 0.0), axis=0, keepdims=True)
            for i in range(count)
        ]
        for i in range(0, count - 1, 2):
            mixed = jnp.where(col >= row, block(i, i), block(i + 1, i + 1))
            out_refs[s][at : at + LANES, :] = mixed.astype(bf16)
            at += LANES
        if count % 2:
            last = block(count - 1, count - 1)
            turned = pltpu.roll(last[half:, :], half, 1)
            mixed = jnp.where(col[:half] >= row[:half], last[:half, :], turned)
            out_refs[s][at : at + half, :] = mixed.astype(bf16)
            at += half
        tail = jnp.zeros((total - top, LANES), f32)
        for i in range(count):
            tail = jnp.where(line == i, diagonals[i], tail)
        trace = sum(diagonals)
        coarse = trace.astype(bf16).astype(f32)
        tail = jnp.where(line == count + 2 * chip, coarse, tail)
        tail = jnp.where(line == count + 2 * chip + 1, trace - coarse, tail)
        out_refs[s][top:, :] = tail.astype(bf16)


def unpack(packed, cols, chips):
    count, crossed = blocks_of(cols)
    top, _ = packed_rows(cols, chips)
    half = LANES // 2
    row, col = grid_of(LANES, LANES)
    tail = packed[top:, :]
    grid = [[None] * count for _ in range(count)]
    at = 0
    for i, j in crossed:
        grid[i][j] = packed[at : at + LANES, :]
        grid[j][i] = grid[i][j].T
        at += LANES
    for i in range(0, count - 1, 2):
        mixed = packed[at : at + LANES, :]
        turned = mixed.T
        grid[i][i] = jnp.where(col >= row, mixed, turned)
        other = jnp.where(col < row, mixed, turned)
        grid[i + 1][i + 1] = jnp.where(col == row, tail[i + 1 : i + 2, :], other)
        at += LANES
    if count % 2:
        i = count - 1
        mixed = packed[at : at + half, :].astype(f32)
        turned = jnp.concatenate([mixed, mixed], axis=0).T
        r, c = row[:half], col[:half]
        upper = jnp.where(c >= r, mixed, turned[:half, :])
        corner = pltpu.roll(jnp.where(c < r, mixed, turned[:half, :]), half, 1)
        corner = jnp.where(c == r + half, tail[i : i + 1, :].astype(f32), corner)
        lower = jnp.where(c < half, turned[half:, :], corner)
        grid[i][i] = jnp.concatenate([upper, lower], axis=0).astype(bf16)
    gram = jnp.concatenate([jnp.concatenate(line, axis=1) for line in grid], axis=0)
    trace = jnp.sum(tail[count : count + 2 * chips, :].astype(f32), keepdims=True)
    return gram, trace


def parts_of(matrix):
    wide = matrix.shape[0] - LANES
    return matrix[:, :wide], matrix[wide:, wide:]


def symmetric_dot(p, q):
    wide = p.shape[0] - LANES
    left = jnp.dot(p, q[:, :wide], preferred_element_type=f32)
    corner = jnp.dot(p[wide:], q[:, wide:], preferred_element_type=f32)
    return left, corner


def completed(parts):
    left, corner = (part.astype(bf16) for part in parts)
    wide = left.shape[1]
    right = [left[wide:, i * LANES : (i + 1) * LANES].T for i in range(wide // LANES)] + [corner]
    return jnp.concatenate([left, jnp.concatenate(right, axis=0)], axis=1)


def writes(blocks, core, out_ref, sem):
    copies = []
    for ref, slots, other in blocks:
        which = 1 - core if other else core
        for k, (base, step) in enumerate(slots):
            copies.append(
                pltpu.make_async_copy(ref.at[k], out_ref.at[0, base + step * which], sem.at[len(copies)])
            )
    return copies


def update_kernel(chips, rows, slots, places, place_ref, counts_ref, *refs):
    n = len(slots)
    mine, told, got = (refs[i * n : (i + 1) * n] for i in range(3))
    held_ref = refs[3 * n]
    out_ref, back_ref = refs[3 * n + 1 :]
    _, strip, cols = held_ref.shape
    core, inner, own_count = place_ref[0], place_ref[2], counts_ref[0]
    a, b, c = poly_first, poly_second, poly_third
    dot = functools.partial(jnp.dot, preferred_element_type=f32)
    span = range(n)
    gram, scale = [], []
    for k in span:
        full, trace = unpack(jnp.where(inner == 1, mine[k][...], told[k][...]), cols, chips)
        gram.append(full)
        scale.append(1.0 / (jnp.sqrt(trace) + 1e-07))
    square = [v * v for v in scale]
    half = range(2)
    first = [[part.astype(f32) for part in parts_of(g)] for g in gram]
    product = [symmetric_dot(g, g) for g in gram]
    poly = [
        completed(
            [(b * square[k]) * first[k][i] + (c * square[k] * square[k]) * product[k][i] for i in half]
        )
        for k in span
    ]
    x = [jnp.concatenate([held_ref[slots[k][0] + core * slots[k][1]], got[k][places[k]]], axis=0) for k in span]
    once = [[square[k] * part for part in symmetric_dot(poly[k], gram[k])] for k in span]
    current = [(a * x[k].astype(f32) + dot(x[k], poly[k])).astype(bf16) for k in span]
    twice = [symmetric_dot(poly[k], completed(once[k])) for k in span]
    second = [
        completed(
            [
                (a * a * square[k]) * first[k][i] + (2.0 * a) * once[k][i] + twice[k][i]
                for i in half
            ]
        )
        for k in span
    ]
    cubic = [dot(current[k], second[k]) for k in span]
    fifth = [dot(cubic[k].astype(bf16), second[k]) for k in span]
    for k in span:
        out = a * current[k].astype(f32) + b * cubic[k] + c * fifth[k]
        live = slots[k][0] + core * slots[k][1] < own_count
        out = jnp.where(live, (math.sqrt(rows) * scale[k]) * out, 0.0).astype(bf16)
        out_ref[k] = out[:strip]
        back_ref[k] = out[strip:]


def join_kernel(ready, place_ref, *refs):
    blocks = [(ref, *block) for ref, block in zip(refs, ready)]
    copies = writes(blocks, place_ref[0], *refs[-2:])
    for copy in copies:
        copy.start()
    for copy in copies:
        copy.wait()


SMEM = pl.BlockSpec(memory_space=pltpu.SMEM)
VMEM = pl.BlockSpec(memory_space=pltpu.VMEM)
ANY = pl.BlockSpec(memory_space=pl.ANY)
HBM = pl.BlockSpec(memory_space=pltpu.HBM)
PARAMS = pltpu.CompilerParams(vmem_limit_bytes=VMEM_LIMIT)


SLOTS = 16
CHUNKS = ((4, 1), (6, 1), (2, 1), (0, 1), (8, 1), (10, 1))
PASSED = {2: (13, -1), 3: (15, -1)}
GROUPS = ((0, -2), (1, 2, -3, 3, 4, 5))
CALLS = ((0, 1, 2, 3), (-2, 4, -3, 5))
LAG = 4


def slot_of(k):
    return CHUNKS[k] if k >= 0 else PASSED[-k]


def sum_grams(grads, counts):
    held = grads[0]
    slots, strip, cols = held.shape
    devices = lax.axis_size("dp")
    chips = devices // CORES
    position = lax.axis_index("dp")
    core, chip = position % CORES, position // CORES
    inner = (chip == 1) | (chip == 2)
    place = jnp.stack([core, chip, inner.astype(jnp.int32)]).astype(jnp.int32)
    _, total = packed_rows(cols, chips)
    chunks = len(CHUNKS)

    def along(pairs):
        return [(CORES * i + k, CORES * j + k) for i, j in pairs for k in range(CORES)]

    swap = [(i, i ^ 1) for i in range(devices)]
    beside = along([(0, 1), (1, 0), (2, 3), (3, 2)])
    across = along([(1, 2), (2, 1)]) + [(i, i ^ 1) for i in (0, 1, devices - 2, devices - 1)]
    partner = [(i, i ^ 1) for i in range(lax.axis_size("expert"))]

    def cost(flops, moved):
        return pl.CostEstimate(flops=int(flops), bytes_accessed=int(moved), transcendentals=0)

    groups = [[slot_of(k) for k in group] for group in GROUPS]
    piece = [jax.ShapeDtypeStruct((len(group), strip, cols), bf16) for group in groups]
    sent = pl.pallas_call(
        functools.partial(split_kernel, groups),
        out_shape=piece,
        in_specs=[SMEM, HBM],
        out_specs=[VMEM] * len(groups),
        scratch_shapes=[pltpu.SemaphoreType.DMA((slots,))],
        compiler_params=PARAMS,
        name="split",
    )(place, pltpu.with_memory_space_constraint(held, pltpu.HBM))
    got, gram, where = [], {}, {}
    for i, group in enumerate(groups):
        size = len(group)
        got.append(lax.ppermute(sent[i], "dp", swap))
        outs = pl.pallas_call(
            functools.partial(gram_kernel, chips, group),
            out_shape=[jax.ShapeDtypeStruct((total, LANES), bf16)] * size,
            in_specs=[SMEM, SMEM, VMEM, VMEM],
            out_specs=[VMEM] * size,
            compiler_params=PARAMS,
            cost_estimate=cost(4 * size * strip * cols * cols, 4 * size * strip * cols),
            name="gram",
        )(place, counts, held, got[i])
        for k, name in enumerate(GROUPS[i]):
            gram[name], where[name] = outs[k], (i, k)
    for k in PASSED:
        came = lax.ppermute(gram[-k], "expert", partner)
        gram[k] = gram[k] + came

    def chosen(one, other):
        return lax.select(jnp.broadcast_to(inner, one.shape), one, other)

    full, told, half = {}, {}, {}
    for t in range(chunks + LAG):
        k = t - LAG
        if k >= 0:
            came = lax.ppermute(half[k], "dp", across)
            full[k] = half[k] + came
        if k < 0:
            load = gram[t]
        elif t < chunks:
            load = chosen(full[k], gram[t])
        else:
            load = full[k]
        came = lax.ppermute(load, "dp", beside)
        if t < chunks:
            half[t] = gram[t] + came
        if k >= 0:
            told[k] = came
    for k in PASSED:
        load = chosen(full[k], told[k])
        full[-k] = told[-k] = lax.ppermute(load, "expert", partner)

    calls = [[slot_of(k) for k in call] for call in CALLS]
    waiting = []
    for i, call in enumerate(CALLS):
        n = len(call)
        out = jax.ShapeDtypeStruct((n, strip, cols), bf16)
        outs = pl.pallas_call(
            functools.partial(
                update_kernel,
                chips,
                strip * devices,
                calls[i],
                [where[k][1] for k in call],
            ),
            out_shape=[out, out],
            in_specs=[SMEM, SMEM] + [VMEM] * (3 * n + 1),
            out_specs=[VMEM, VMEM],
            compiler_params=PARAMS,
            cost_estimate=cost(8 * n * cols**3 + 8 * n * strip * cols * cols, 8 * n * strip * cols),
            name="update",
        )(
            place,
            counts,
            *[full[k] for k in call],
            *[told[k] for k in call],
            *[got[where[k][0]] for k in call],
            held,
        )
        came = lax.ppermute(outs[1], "dp", swap)
        waiting += [(outs[0], calls[i], False), (came, calls[i], True)]
    return pl.pallas_call(
        functools.partial(join_kernel, [block[1:] for block in waiting]),
        out_shape=jax.ShapeDtypeStruct((1,) + held.shape, bf16),
        in_specs=[SMEM] + [VMEM] * len(waiting),
        out_specs=HBM,
        scratch_shapes=[pltpu.SemaphoreType.DMA((slots,))],
        compiler_params=PARAMS,
        name="join",
    )(place, *[block[0] for block in waiting])


def solution(mesh):
    placed = (P("expert", None, "dp", None), P("expert"))
    devices = mesh.shape["dp"]

    def step(grads, counts):
        _, slots, rows, cols = grads.shape
        strip = rows // devices
        summed = devices == 4 * CORES and cols % LANES == 0 and slots == SLOTS and mesh.shape["expert"] % 2 == 0
        summed = summed and CORES * strip * cols >= packed_rows(cols, devices // CORES)[1] * LANES

        def per_device(grads, counts):
            return (sum_grams if summed else strips_to_owners)(grads, counts)

        mapped = jax.shard_map(
            per_device,
            mesh=mesh,
            in_specs=placed,
            out_specs=P("expert", None, "dp", None),
            check_vma=False,
        )
        return mapped(grads, counts)

    return step
```
